128 devices in a mesh: dom: 16 (over y, z), sub: 8 (over x, core).
Axes of the slice: x: 4, y: 4, z: 4, core: 2. Of those that a mesh axis runs over, the one named last changes fastest.
Arguments:
- features: bfloat16 [131072, 256], P(('dom', 'sub')), may hold values from -6 to 6
- cotangent: bfloat16 [131072, 256], P(('dom', 'sub')), may hold values from -6 to 6
- w_self_one: bfloat16 [256, 256], replicated, may hold values from -0.375 to 0.375
- w_nbr_one: bfloat16 [256, 256], replicated, may hold values from -0.375 to 0.375
- bias_one: float32 [256], replicated, may hold values from -4 to 4
- w_self_two: bfloat16 [256, 256], replicated, may hold values from -0.375 to 0.375
- w_nbr_two: bfloat16 [256, 256], replicated, may hold values from -0.375 to 0.375
- in_count: int32 [131072], P(('dom', 'sub')), may hold values from 0 to 7
- send_list: int32 [128, 128, 4], P(('dom', 'sub')), may hold values from 0 to 1023
- src_slot: int32 [128, 2048], P(('dom', 'sub')), may hold values from 0 to 1535
- dst_slot: int32 [128, 2048], P(('dom', 'sub')), may hold values from 0 to 1535
- edge_count: int32 [128], P(('dom', 'sub')), may hold values from 512 to 2048, as said below
Outputs:
- grad_features: bfloat16 [131072, 256], P(('dom', 'sub'))
- grad_weights: float32 [4, 256, 256], replicated
- grad_bias: float32 [256], replicated
The draws below stay inside these ranges and needn't reach their ends.
Inputs may be any that keep to these rules, and one draw needn't show every extreme that they name: Each device's first edge_count slots are live; one device has all 2048 live in every draw.
All inputs are finite; a program needn't handle non-finite values.
Results may differ from the reference program's by a relative error of at most 0.0056.
Values may be sent and summed in bfloat16 or wider, within the bound.
A program may use at most 64 MiB of HBM per device.

```python
import jax
import jax.numpy as jnp
from jax import lax

D = 256
NODE_DEV = 1024
CAP = 4
E_DEV = 2048
DEV_COUNT = 128
NODES = 131072
SLOTS = 1536
N_DOM = 16
N_SUB = 8


def draw_edge_count(key, part):
    first_key, second_key = jax.random.split(jax.random.fold_in(key, 17))
    counts = jax.random.randint(first_key, (N_DOM * N_SUB,), E_DEV // 4, E_DEV + 1)
    fullest = jax.random.randint(second_key, (), 0, N_DOM * N_SUB)
    return jnp.where(jnp.arange(N_DOM * N_SUB) == fullest, E_DEV, counts).astype(jnp.int32)


def set_ends(result, key, least, high):
    index_at = [jax.random.randint(jax.random.fold_in(key, axis), (), 0, length) for axis, length in enumerate(result.shape)]
    main_axis = result.shape.index(max(result.shape))
    neighbour = index_at[:main_axis] + [(index_at[main_axis] + 1) % result.shape[main_axis]] + index_at[main_axis + 1:]
    return result.at[tuple(index_at)].set(least).at[tuple(neighbour)].set(high)


def level_of(stream_key, extent, cuts, least, top_value):
    def one(dim, parts):
        steps = jax.random.uniform(jax.random.fold_in(jax.random.fold_in(stream_key, 6), dim), (parts,), jnp.float32, least / len(cuts), top_value / len(cuts))
        return jnp.repeat(jnp.exp(steps), extent[dim] // parts).reshape((-1,) + (1,) * (len(extent) - dim - 1))

    gain = one(*cuts[0])
    for cut in cuts[1:]:
        gain = gain * one(*cut)
    return gain


def centred(key, dims, scale, bound, cuts=(), held_as=jnp.bfloat16):
    values = scale * jax.random.normal(key, dims, jnp.float32)
    if cuts:
        values = values * level_of(key, dims, cuts, -0.22, 0.18)
    return jnp.clip(values, -bound, bound).astype(held_as)


def setup_inputs(seed: int = 0) -> dict:
    key_of = jax.random.split(jax.random.key(seed), 13)
    return {
        "features": centred(key_of[0], (NODES, D), 1.0, 6.0, ((0, 128),)),
        "cotangent": centred(key_of[1], (NODES, D), 1.0, 6.0, ((0, 128),)),
        "w_self_one": centred(key_of[2], (D, D), D ** -0.5, 0.375),
        "w_nbr_one": centred(key_of[3], (D, D), D ** -0.5, 0.375),
        "bias_one": centred(key_of[4], (D,), 0.7, 4.0, (), jnp.float32),
        "w_self_two": centred(key_of[5], (D, D), D ** -0.5, 0.375),
        "w_nbr_two": centred(key_of[6], (D, D), D ** -0.5, 0.375),
        "in_count": set_ends(jax.random.randint(key_of[7], (NODES,), 0, 8), jax.random.fold_in(key_of[7], 1), 0, 7).astype(jnp.int32),
        "send_list": set_ends(jax.random.randint(key_of[8], (DEV_COUNT, DEV_COUNT, CAP), 0, NODE_DEV), jax.random.fold_in(key_of[8], 1), 0, NODE_DEV - 1).astype(jnp.int32),
        "src_slot": set_ends(jax.random.randint(key_of[9], (DEV_COUNT, E_DEV), 0, SLOTS), jax.random.fold_in(key_of[9], 1), 0, SLOTS - 1).astype(jnp.int32),
        "dst_slot": set_ends(jax.random.randint(key_of[10], (DEV_COUNT, E_DEV), 0, SLOTS), jax.random.fold_in(key_of[10], 1), 0, SLOTS - 1).astype(jnp.int32),
        "edge_count": draw_edge_count(jax.random.fold_in(key_of[12], 71), 0),
    }


def global_nodes(slot, send_list):
    device_ids = jnp.arange(N_DOM * N_SUB, dtype=jnp.int32)[:, None]
    mirror_pos = jnp.clip(slot - NODE_DEV, 0, N_DOM * N_SUB * CAP - 1)
    owner_dev = mirror_pos // CAP
    within = mirror_pos % CAP
    remote = owner_dev * NODE_DEV + send_list[owner_dev, device_ids, within]
    return jnp.where(slot < NODE_DEV, device_ids * NODE_DEV + slot, remote).astype(jnp.int32)

def spread(values, from_node, into_node, live_mask, nodes):

    def one_device(total, pieces):
        from_row, into_row, live_row = pieces
        picked = jnp.where(live_row[:, None], values[from_row].astype(jnp.float32), 0.0)
        return (total.at[into_row].add(picked), None)
    start = jnp.zeros((nodes, values.shape[1]), jnp.float32)
    total, _ = lax.scan(one_device, start, (from_node, into_node, live_mask))
    return total

def silu_grad(value):
    sig = jax.nn.sigmoid(value)
    return sig * (1.0 + value * (1.0 - sig))

def tdot(left, right):
    return jnp.dot(left.T, right, preferred_element_type=jnp.float32)

def reference(features, cotangent, w_self_one, w_nbr_one, bias_one, w_self_two, w_nbr_two, in_count, send_list, src_slot, dst_slot, edge_count):
    nodes = features.shape[0]
    sources = global_nodes(src_slot, send_list)
    targets = global_nodes(dst_slot, send_list)
    live_mask = jnp.arange(E_DEV, dtype=jnp.int32)[None, :] < edge_count[:, None]
    inverse = (1.0 / jnp.maximum(in_count, 1).astype(jnp.float32))[:, None]
    mean_one = (spread(features, sources, targets, live_mask, nodes) * inverse).astype(jnp.bfloat16)
    z_one = jnp.dot(features, w_self_one, preferred_element_type=jnp.float32) + jnp.dot(mean_one, w_nbr_one, preferred_element_type=jnp.float32) + bias_one
    h_one = jax.nn.silu(z_one).astype(jnp.bfloat16)
    mean_two = (spread(h_one, sources, targets, live_mask, nodes) * inverse).astype(jnp.bfloat16)
    message_two = (jnp.dot(cotangent, w_nbr_two.T, preferred_element_type=jnp.float32) * inverse).astype(jnp.bfloat16)
    grad_h_one = jnp.dot(cotangent, w_self_two.T, preferred_element_type=jnp.float32) + spread(message_two, targets, sources, live_mask, nodes)
    grad_z_one = (grad_h_one * silu_grad(z_one)).astype(jnp.bfloat16)
    message_one = (jnp.dot(grad_z_one, w_nbr_one.T, preferred_element_type=jnp.float32) * inverse).astype(jnp.bfloat16)
    grad_features = (jnp.dot(grad_z_one, w_self_one.T, preferred_element_type=jnp.float32) + spread(message_one, targets, sources, live_mask, nodes)).astype(jnp.bfloat16)
    norm_factor = jnp.float32(nodes) ** (-0.5)
    grad_weights = jnp.stack([tdot(features, grad_z_one), tdot(mean_one, grad_z_one), tdot(h_one, cotangent), tdot(mean_two, cotangent)]) * norm_factor
    grad_bias = lax.optimization_barrier(jnp.sum(grad_z_one.astype(jnp.float32), axis=0)) * norm_factor
    return (grad_features, grad_weights, grad_bias)
```

```python
import functools

import jax
import jax.numpy as jnp
from jax import lax
from jax.experimental import pallas as pl
from jax.experimental.pallas import tpu as pltpu
from jax.sharding import PartitionSpec as P

MESH = pl.DeviceIdType.MESH
F32 = jnp.float32
BF16 = jnp.bfloat16
ONE_HOT = jnp.float8_e4m3fn


def nn(left, right):
    return jnp.dot(left, right, preferred_element_type=F32)


def tn(left, right):
    return lax.dot_general(left, right, (((0,), (0,)), ((), ())), preferred_element_type=F32)


def nt(left, right):
    return lax.dot_general(left, right, (((1,), (1,)), ((), ())), preferred_element_type=F32)


def kernel(
    n_dom,
    n_sub,
    norm_factor,
    count_ref,
    src_ref,
    dst_ref,
    send_ref,
    in_count_ref,
    bias_ref,
    feat_hbm,
    cot_hbm,
    ws1_hbm,
    wn1_hbm,
    ws2_hbm,
    wn2_hbm,
    gfeat_hbm,
    gw_hbm,
    gb_ref,
    feat,
    cot,
    wts,
    src_hot,
    dst_hot,
    adj,
    place,
    inv,
    ybuf,
    zbuf,
    gbuf,
    fown,
    gown,
    hown,
    mbuf,
    hbuf,
    gzbuf,
    send1,
    recv1,
    send2,
    recv2,
    send3,
    recv3,
    send4,
    recv4,
    wpart,
    bpart,
    wpair,
    bpair,
    bsum,
    brecv,
    rs_send,
    rs_recv,
    ag_send,
    ag_all,
    obuf,
    gwbuf,
    in_sem,
    loc_sem,
    ssem,
    rsem,
    out_sem,
):
    nodes, dim = feat.shape
    n_dev = n_dom * n_sub
    n_chip = n_dev // 2
    n_mir = place.shape[1]
    slots = nodes + n_mir
    per_peer = n_mir // n_dev
    half = wpair.shape[0]
    blk = 256
    d = lax.axis_index("dom")
    s = lax.axis_index("sub")
    me = d * n_sub + s
    chip = me // 2
    core = lax.rem(me, 2)
    partner = (d, s + 1 - 2 * core)

    loads = [
        pltpu.make_async_copy(a, b, in_sem.at[i])
        for i, (a, b) in enumerate(
            [
                (feat_hbm, feat),
                (cot_hbm, cot),
                (ws1_hbm, wts.at[0]),
                (wn1_hbm, wts.at[1]),
                (ws2_hbm, wts.at[2]),
                (wn2_hbm, wts.at[3]),
            ]
        )
    ]
    for c in loads:
        c.start()

    def at(p):
        return (p // n_sub, lax.rem(p, n_sub))

    barrier = pltpu.get_barrier_semaphore()

    def greet(i, _):
        pl.semaphore_signal(barrier, 1, device_id=at(lax.rem(me + i, n_dev)), device_id_type=MESH)
        return 0

    lax.fori_loop(1, n_dev, greet, 0)

    def exchange(send, recv, k):
        def one(i, _):
            p = lax.rem(me + i, n_dev)
            pltpu.make_async_remote_copy(
                src_ref=send.at[p],
                dst_ref=recv.at[me],
                send_sem=ssem.at[k],
                recv_sem=rsem.at[k],
                device_id=at(p),
                device_id_type=MESH,
            ).start()
            return 0

        lax.fori_loop(1, n_dev, one, 0)
        pltpu.make_async_copy(send.at[me], recv.at[me], loc_sem.at[k]).start()

    def arrive(send, recv, k):
        pltpu.make_async_copy(send.at[me], recv.at[me], loc_sem.at[k]).wait()
        all_in = recv.at[pl.ds(0, n_dev - 1)]
        pltpu.make_async_copy(all_in, all_in, rsem.at[k]).wait()

    def sent(send, k):
        all_out = send.at[pl.ds(0, n_dev - 1)]
        pltpu.make_async_copy(all_out, all_out, ssem.at[k]).wait()

    def rows(ref, i):
        return ref.at[pl.ds(pl.multiple_of(i * blk, blk), blk), :]

    def mir(ref):
        return ref.reshape(n_mir, dim)

    place[...] = (
        lax.broadcasted_iota(jnp.int32, (nodes, n_mir), 0) == send_ref[...]
    ).astype(BF16)
    inv_row = 1.0 / jnp.maximum(in_count_ref[...], 1).astype(F32)
    inv_col = jnp.broadcast_to(inv_row, (128, nodes)).T
    inv[...] = jnp.concatenate([inv_col] * (dim // 128), axis=1)
    loads[0].wait()
    loads[1].wait()
    ybuf[...] = (cot[...].astype(F32) * inv[...]).astype(BF16)
    send1[:, 0] = tn(place[...], feat[...]).astype(BF16).reshape(n_dev, per_peer, dim)
    send1[:, 1] = tn(place[...], ybuf[...]).astype(BF16).reshape(n_dev, per_peer, dim)

    pl.semaphore_wait(barrier, n_dev - 1)
    exchange(send1, recv1, 0)

    edges = src_ref.shape[1]
    live = lax.broadcasted_iota(jnp.int32, (1, edges), 1) < count_ref[0]
    src_row = jnp.where(live, src_ref[...], -1)
    dst_row = jnp.where(live, dst_ref[...], -1)

    def hot(i, _):
        ids = lax.broadcasted_iota(jnp.int32, (blk, edges), 0) + i * blk
        rows(src_hot, i)[...] = (ids == src_row).astype(ONE_HOT)
        rows(dst_hot, i)[...] = (ids == dst_row).astype(ONE_HOT)
        return 0

    lax.fori_loop(0, slots // blk, hot, 0)

    def build(i, _):
        rows(adj, i)[...] = nt(rows(dst_hot, i)[...], src_hot[...]).astype(BF16)
        return 0

    lax.fori_loop(0, slots // blk, build, 0)

    fown[...] = nn(adj[:, :nodes], feat[...])
    gown[...] = tn(adj[:nodes, :], ybuf[...])
    for c in loads[2:]:
        c.wait()

    arrive(send1, recv1, 0)
    fm = mir(recv1[:, 0])
    gm = mir(recv1[:, 1])
    send2[:, 0] = (
        (fown[nodes:, :] + nn(adj[nodes:, nodes:], fm)).astype(BF16).reshape(n_dev, per_peer, dim)
    )
    send2[:, 1] = (
        (gown[nodes:, :] + tn(adj[nodes:, nodes:], gm)).astype(BF16).reshape(n_dev, per_peer, dim)
    )
    exchange(send2, recv2, 1)
    fown[:nodes, :] += nn(adj[:nodes, nodes:], fm)
    gown[:nodes, :] += tn(adj[nodes:, :nodes], gm)
    zbuf[...] = nn(feat[...], wts[0]) + bias_ref[...]
    gbuf[...] = nt(cot[...], wts[2])

    arrive(send2, recv2, 1)
    fm2 = mir(recv2[:, 0])
    gm2 = mir(recv2[:, 1])

    def dense(i, acc):
        r = pl.multiple_of(i * blk, blk)
        here = pl.ds(r, blk)
        pick = place[here, :]
        scale = inv[here, :]
        mean = ((fown[here, :] + nn(pick, fm2)) * scale).astype(BF16)
        gsum = (gown[here, :] + nn(pick, gm2)).astype(BF16)
        mbuf[here, :] = mean
        gown[here, :] = gsum.astype(F32)
        z = zbuf[here, :] + nn(mean, wts[1])
        gh = gbuf[here, :] + nt(gsum, wts[3])
        sig = 1.0 / (1.0 + jnp.exp(-z))
        hbuf[here, :] = (z * sig).astype(BF16)
        gz = (gh * (sig * (1.0 + z * (1.0 - sig)))).astype(BF16)
        gzbuf[here, :] = gz
        gzf = gz.astype(F32)
        ybuf[here, :] = (gzf * scale).astype(BF16)
        return acc + jnp.sum(gzf, axis=0, keepdims=True)

    bpart[...] = lax.fori_loop(0, nodes // blk, dense, jnp.zeros((1, dim), F32))

    send3[...] = tn(place[...], ybuf[...]).astype(BF16).reshape(n_dev, per_peer, dim)
    exchange(send3, recv3, 2)

    wpart[pl.ds(0, dim), :] = tn(feat[...], gzbuf[...])
    wpart[pl.ds(dim, dim), :] = tn(mbuf[...], gzbuf[...])
    wpart[pl.ds(2 * dim, dim), :] = tn(hbuf[...], cot[...])
    wpart[pl.ds(3 * dim, dim), :] = tn(hbuf[...], gown[:nodes, :].astype(BF16))
    mine = pl.ds(pl.multiple_of(core * half, half), half)
    other = pl.ds(pl.multiple_of((1 - core) * half, half), half)
    pair_w = pltpu.make_async_remote_copy(
        src_ref=wpart.at[other, :],
        dst_ref=wpair,
        send_sem=ssem.at[4],
        recv_sem=rsem.at[4],
        device_id=partner,
        device_id_type=MESH,
    )
    pair_b = pltpu.make_async_remote_copy(
        src_ref=bpart,
        dst_ref=bpair,
        send_sem=ssem.at[5],
        recv_sem=rsem.at[5],
        device_id=partner,
        device_id_type=MESH,
    )
    pair_w.start()
    pair_b.start()

    hown[...] = tn(adj[:nodes, :], ybuf[...])

    pair_w.wait()
    pair_b.wait()
    rs_send[...] = (wpart[mine, :] + wpair[...]).astype(rs_send.dtype).reshape(n_chip, 8, dim)
    bsum[...] = bpart[...] + bpair[...]

    def scatter(i, _):
        q = lax.rem(chip + i, n_chip)
        to = at(q * 2 + core)
        pltpu.make_async_remote_copy(
            src_ref=rs_send.at[q],
            dst_ref=rs_recv.at[chip],
            send_sem=ssem.at[6],
            recv_sem=rsem.at[6],
            device_id=to,
            device_id_type=MESH,
        ).start()
        pltpu.make_async_remote_copy(
            src_ref=bsum,
            dst_ref=brecv.at[chip],
            send_sem=ssem.at[7],
            recv_sem=rsem.at[7],
            device_id=to,
            device_id_type=MESH,
        ).start()
        return 0

    lax.fori_loop(1, n_chip, scatter, 0)
    own_rs = pltpu.make_async_copy(rs_send.at[chip], rs_recv.at[chip], loc_sem.at[4])
    own_rs.start()
    own_b = pltpu.make_async_copy(bsum, brecv.at[chip], loc_sem.at[5])
    own_b.start()

    arrive(send3, recv3, 2)
    hm = mir(recv3[...])
    send4[...] = (
        (hown[nodes:, :] + tn(adj[nodes:, nodes:], hm)).astype(BF16).reshape(n_dev, per_peer, dim)
    )
    exchange(send4, recv4, 3)
    hown[:nodes, :] += tn(adj[nodes:, :nodes], hm)
    zbuf[...] = nt(gzbuf[...], wts[0])

    own_rs.wait()
    own_b.wait()
    others = rs_recv.at[pl.ds(0, n_chip - 1)]
    pltpu.make_async_copy(others, others, rsem.at[6]).wait()
    others = brecv.at[pl.ds(0, n_chip - 1)]
    pltpu.make_async_copy(others, others, rsem.at[7]).wait()
    ag_send[...] = (jnp.sum(rs_recv[...].astype(F32), axis=0) * norm_factor).astype(ag_send.dtype)
    gb_ref[...] = jnp.sum(brecv[...], axis=0) * norm_factor

    def gather(i, _):
        q = lax.rem(chip + i, n_chip)
        pltpu.make_async_remote_copy(
            src_ref=ag_send,
            dst_ref=ag_all.at[core, chip],
            send_sem=ssem.at[8],
            recv_sem=rsem.at[8],
            device_id=at(q * 2 + core),
            device_id_type=MESH,
        ).start()
        return 0

    lax.fori_loop(1, n_chip, gather, 0)
    own_ag = pltpu.make_async_copy(ag_send, ag_all.at[core, chip], loc_sem.at[6])
    own_ag.start()

    arrive(send4, recv4, 3)
    hm2 = mir(recv4[...])

    def last(i, _):
        here = pl.ds(pl.multiple_of(i * blk, blk), blk)
        hsum = (hown[here, :] + nn(place[here, :], hm2)).astype(BF16)
        obuf[here, :] = (zbuf[here, :] + nt(hsum, wts[1])).astype(BF16)
        return 0

    lax.fori_loop(0, nodes // blk, last, 0)
    put = pltpu.make_async_copy(obuf, gfeat_hbm, out_sem.at[0])
    put.start()

    own_ag.wait()
    others = ag_all.at[core, pl.ds(0, n_chip - 1)]
    pltpu.make_async_copy(others, others, rsem.at[8]).wait()
    swap = pltpu.make_async_remote_copy(
        src_ref=ag_all.at[core],
        dst_ref=ag_all.at[core],
        send_sem=ssem.at[9],
        recv_sem=rsem.at[9],
        device_id=partner,
        device_id_type=MESH,
    )
    swap.start()
    swap.wait()
    gwbuf[...] = ag_all[...].astype(F32).reshape(4 * dim, dim)
    put_w = pltpu.make_async_copy(gwbuf, gw_hbm, out_sem.at[1])
    put_w.start()

    sent(send1, 0)
    sent(send2, 1)
    sent(send3, 2)
    sent(send4, 3)
    for ref, k in ((rs_send, 6), (brecv, 7)):
        others = ref.at[pl.ds(0, n_chip - 1)]
        pltpu.make_async_copy(others, others, ssem.at[k]).wait()
    others = ag_all.at[core, pl.ds(0, n_chip - 1)]
    pltpu.make_async_copy(others, others, ssem.at[8]).wait()
    put.wait()
    put_w.wait()


def shards(
    n_dom,
    n_sub,
    features,
    cotangent,
    w_self_one,
    w_nbr_one,
    bias_one,
    w_self_two,
    w_nbr_two,
    in_count,
    send_list,
    src_slot,
    dst_slot,
    edge_count,
):
    nodes, dim = features.shape
    n_dev = n_dom * n_sub
    n_chip = n_dev // 2
    per_peer = send_list.shape[2]
    n_mir = n_dev * per_peer
    slots = nodes + n_mir
    edges = src_slot.shape[1]
    vm = pl.BlockSpec(memory_space=pltpu.VMEM)
    sm = pl.BlockSpec(memory_space=pltpu.SMEM)
    hbm = pl.BlockSpec(memory_space=pl.ANY)
    norm_factor = float(nodes * n_dev) ** -0.5
    msg2 = pltpu.VMEM((n_dev, 2, per_peer, dim), BF16)
    msg1 = pltpu.VMEM((n_dev, per_peer, dim), BF16)
    full = pltpu.VMEM((nodes, dim), F32)
    fullb = pltpu.VMEM((nodes, dim), BF16)
    allf = pltpu.VMEM((slots, dim), F32)
    rs_t = BF16
    ag_t = BF16
    gfeat, gw, gb = pl.pallas_call(
        functools.partial(kernel, n_dom, n_sub, norm_factor),
        out_shape=(
            jax.ShapeDtypeStruct((nodes, dim), BF16),
            jax.ShapeDtypeStruct((4 * dim, dim), F32),
            jax.ShapeDtypeStruct((1, dim), F32),
        ),
        in_specs=[sm, vm, vm, vm, vm, vm, hbm, hbm, hbm, hbm, hbm, hbm],
        out_specs=(hbm, hbm, vm),
        scratch_shapes=[
            fullb,
            fullb,
            pltpu.VMEM((4, dim, dim), BF16),
            pltpu.VMEM((slots, edges), ONE_HOT),
            pltpu.VMEM((slots, edges), ONE_HOT),
            pltpu.VMEM((slots, slots), BF16),
            pltpu.VMEM((nodes, n_mir), BF16),
            full,
            fullb,
            full,
            full,
            allf,
            allf,
            allf,
            fullb,
            fullb,
            fullb,
            msg2,
            msg2,
            msg2,
            msg2,
            msg1,
            msg1,
            msg1,
            msg1,
            pltpu.VMEM((4 * dim, dim), F32),
            pltpu.VMEM((1, dim), F32),
            pltpu.VMEM((2 * dim, dim), F32),
            pltpu.VMEM((1, dim), F32),
            pltpu.VMEM((1, dim), F32),
            pltpu.VMEM((n_chip, 1, dim), F32),
            pltpu.VMEM((n_chip, 2 * dim // n_chip, dim), rs_t),
            pltpu.VMEM((n_chip, 2 * dim // n_chip, dim), rs_t),
            pltpu.VMEM((2 * dim // n_chip, dim), ag_t),
            pltpu.VMEM((2, n_chip, 2 * dim // n_chip, dim), ag_t),
            fullb,
            pltpu.VMEM((4 * dim, dim), F32),
            pltpu.SemaphoreType.DMA((6,)),
            pltpu.SemaphoreType.DMA((7,)),
            pltpu.SemaphoreType.DMA((10,)),
            pltpu.SemaphoreType.DMA((10,)),
            pltpu.SemaphoreType.DMA((2,)),
        ],
        compiler_params=pltpu.CompilerParams(
            collective_id=0, has_side_effects=True, vmem_limit_bytes=60 << 20
        ),
    )(
        edge_count,
        src_slot,
        dst_slot,
        send_list.reshape(1, n_mir),
        in_count.reshape(1, nodes),
        bias_one.reshape(1, dim),
        features,
        cotangent,
        w_self_one,
        w_nbr_one,
        w_self_two,
        w_nbr_two,
    )
    return gfeat, gw.reshape(4, dim, dim), gb.reshape(dim)


def solution(mesh):
    both = ("dom", "sub")
    return jax.shard_map(
        functools.partial(shards, mesh.shape["dom"], mesh.shape["sub"]),
        mesh=mesh,
        in_specs=(
            P(both, None),
            P(both, None),
            P(),
            P(),
            P(),
            P(),
            P(),
            P(both),
            P(both, None, None),
            P(both, None),
            P(both, None),
            P(both),
        ),
        out_specs=(P(both, None), P(), P()),
        check_vma=False,
    )
```

```python
import contextlib
import functools

import jax
import jax.numpy as jnp
from jax import lax
from jax.experimental import pallas as pl
from jax.experimental.pallas import tpu as pltpu
from jax.sharding import PartitionSpec as P

MESH = pl.DeviceIdType.MESH
F32 = jnp.float32
BF16 = jnp.bfloat16
ONE_HOT = jnp.float8_e4m3fn
FAR = (10, 9, 11, 6, 14, 8, 2, 5, 7, 13, 15, 4, 12, 1, 3)


def scope(name):
    return contextlib.nullcontext()


def nn(left, right):
    return jnp.dot(left, right, preferred_element_type=F32)


def tn(left, right):
    return lax.dot_general(left, right, (((0,), (0,)), ((), ())), preferred_element_type=F32)


def nt(left, right):
    return lax.dot_general(left, right, (((1,), (1,)), ((), ())), preferred_element_type=F32)


def digits(codes):
    total = 0
    for code in reversed(codes):
        total = total * 16 + code
    return total


def wrap4(v):
    return jnp.where(v >= 4, v - 4, v)


def kernel(
    n_dom,
    n_sub,
    norm_factor,
    count_hbm,
    src_hbm,
    dst_hbm,
    send_hbm,
    in_count_hbm,
    bias_hbm,
    feat_hbm,
    cot_hbm,
    ws1_hbm,
    wn1_hbm,
    ws2_hbm,
    wn2_hbm,
    gfeat_ref,
    gw_ref,
    gb_ref,
    count_ref,
    src_ref,
    dst_ref,
    send_ref,
    in_count_ref,
    bias_ref,
    feat,
    cot,
    wts,
    src_hot,
    dst_hot,
    adj,
    place,
    inv,
    ybuf,
    zbuf,
    gbuf,
    fown,
    gown,
    hown,
    mbuf,
    hbuf,
    gzbuf,
    sends,
    recvs,
    wpart,
    bpart,
    wpair,
    bpair,
    bsum,
    brecv,
    rs_send,
    rs_recv,
    ag_send,
    ag_all,
    in_sem,
    loc_sem,
    ssem,
    rsem,
):
    nodes, dim = feat.shape
    n_dev = n_dom * n_sub
    n_chip = n_dev // 2
    n_mir = place.shape[1]
    slots = nodes + n_mir
    per_peer = n_mir // n_dev
    half = wpair.shape[0]
    blk = 256
    d = lax.axis_index("dom")
    s = lax.axis_index("sub")
    me = d * n_sub + s
    chip = lax.div(me, 2)
    core = lax.rem(me, 2)
    at_y, at_z, at_x = lax.div(d, 4), lax.rem(d, 4), lax.div(s, 2)
    partner = (d, s + 1 - 2 * core)

    small = [
        (send_hbm, send_ref),
        (in_count_hbm, in_count_ref),
        (count_hbm, count_ref),
        (src_hbm, src_ref),
        (dst_hbm, dst_ref),
        (bias_hbm, bias_ref),
    ]
    large = [
        (feat_hbm, feat),
        (cot_hbm, cot),
        (ws1_hbm, wts.at[0]),
        (wn1_hbm, wts.at[1]),
        (ws2_hbm, wts.at[2]),
        (wn2_hbm, wts.at[3]),
    ]
    loads = [
        pltpu.make_async_copy(a, b, in_sem.at[i]) for i, (a, b) in enumerate(small + large)
    ]
    for c in loads:
        c.start()

    xs = [wrap4(at_x + k) * 2 for k in (2, 1, 3, 0)]
    cores = [1 - core, core]

    def each(do, both):
        def line(dom, is_mine):
            for k in range(4):
                for j in range(2):
                    if (both or j == 1) and not (is_mine and k == 3 and j == 1):
                        do(dom, xs[k] + cores[j])

        def dom_of(code):
            return wrap4(at_y + lax.div(code, 4)) * 4 + wrap4(at_z + lax.rem(code, 4))

        def turn(_, left):
            line(dom_of(lax.rem(left, 16)), False)
            return lax.div(left, 16)

        lax.fori_loop(0, 7, turn, jnp.int32(digits(FAR[:7])))
        lax.fori_loop(0, 7, turn, jnp.int32(digits(FAR[7:14])))
        line(dom_of(jnp.int32(FAR[14])), False)
        line(d, True)

    barrier = pltpu.get_barrier_semaphore()
    with scope("greet"):
        each(
            lambda a, b: pl.semaphore_signal(barrier, 1, device_id=(a, b), device_id_type=MESH),
            True,
        )

    def exchange(k):
        def one(a, b):
            pltpu.make_async_remote_copy(
                src_ref=sends.at[k, a * n_sub + b],
                dst_ref=recvs.at[k, me],
                send_sem=ssem.at[k],
                recv_sem=rsem.at[k],
                device_id=(a, b),
                device_id_type=MESH,
            ).start()

        with scope(f"ex{k}"):
            each(one, True)
            pltpu.make_async_copy(sends.at[k, me], recvs.at[k, me], loc_sem.at[k]).start()

    def arrive(k):
        with scope(f"arr{k}"):
            pltpu.make_async_copy(sends.at[k, me], recvs.at[k, me], loc_sem.at[k]).wait()
            all_in = recvs.at[k, pl.ds(0, n_dev - 1)]
            pltpu.make_async_copy(all_in, all_in, rsem.at[k]).wait()
        return recvs[k].reshape(n_mir, dim)

    def sent(k):
        all_out = sends.at[k, pl.ds(0, n_dev - 1)]
        pltpu.make_async_copy(all_out, all_out, ssem.at[k]).wait()

    def rows(ref, i):
        return ref.at[pl.ds(pl.multiple_of(i * blk, blk), blk), :]

    def fill(k, value):
        sends[k] = value.astype(BF16).reshape(n_dev, per_peer, dim)

    with scope("prep"):
        loads[0].wait()
        loads[1].wait()
        lists = send_ref[...]
        parts = jnp.concatenate([lists // 32, lists % 32], axis=0).astype(F32).astype(BF16)
        lane = lax.broadcasted_iota(jnp.int32, (n_dev, n_mir), 1)
        widen = (
            lax.shift_right_logical(lane, 2) == lax.broadcasted_iota(jnp.int32, (n_dev, n_mir), 0)
        ).astype(BF16)
        wide = nn(parts, widen)
        wide = wide[:per_peer] * 32.0 + wide[per_peer:]
        turn_of = lax.broadcasted_iota(jnp.int32, (per_peer, n_mir), 1) & 3
        mine_of = turn_of == lax.broadcasted_iota(jnp.int32, (per_peer, n_mir), 0)
        picked = jnp.sum(jnp.where(mine_of, wide, 0.0), axis=0, keepdims=True).astype(jnp.int32)
        place[...] = (lax.broadcasted_iota(jnp.int32, (nodes, n_mir), 0) == picked).astype(BF16)
        inv_row = 1.0 / jnp.maximum(in_count_ref[...], 1).astype(F32)
        inv_col = jnp.broadcast_to(inv_row, (128, nodes)).T
        inv[...] = jnp.concatenate([inv_col] * (dim // 128), axis=1)
        loads[6].wait()
        fill(0, tn(place[...], feat[...]))
        loads[7].wait()
        ybuf[...] = (cot[...].astype(F32) * inv[...]).astype(BF16)
        fill(1, tn(place[...], ybuf[...]))

    with scope("hot"):
        for c in loads[2:6]:
            c.wait()
        edges = src_ref.shape[1]
        live = lax.broadcasted_iota(jnp.int32, (1, edges), 1) < count_ref[...]
        src_row = jnp.where(live, src_ref[...], -1)
        dst_row = jnp.where(live, dst_ref[...], -1)

        def hot(i, _):
            ids = lax.broadcasted_iota(jnp.int32, (blk, edges), 0) + i * blk
            rows(src_hot, i)[...] = (ids == src_row).astype(ONE_HOT)
            rows(dst_hot, i)[...] = (ids == dst_row).astype(ONE_HOT)
            return 0

        lax.fori_loop(0, slots // blk, hot, 0)

    with scope("bwait"):
        pl.semaphore_wait(barrier, n_dev - 1)
    exchange(0)
    exchange(1)

    with scope("build"):

        def build(i, _):
            rows(adj, i)[...] = nt(rows(dst_hot, i)[...], src_hot[...]).astype(BF16)
            return 0

        lax.fori_loop(0, slots // blk, build, 0)

    with scope("own1"):
        fown[...] = nn(adj[:, :nodes], feat[...])
        gown[...] = tn(adj[:nodes, :], ybuf[...])
        for c in loads[8:]:
            c.wait()

    fm = arrive(0)
    fill(2, fown[nodes:, :] + nn(adj[nodes:, nodes:], fm))
    exchange(2)
    gm = arrive(1)
    fill(3, gown[nodes:, :] + tn(adj[nodes:, nodes:], gm))
    exchange(3)
    with scope("own2"):
        fown[:nodes, :] += nn(adj[:nodes, nodes:], fm)
        gown[:nodes, :] += tn(adj[nodes:, :nodes], gm)
        zbuf[...] = nn(feat[...], wts[0]) + bias_ref[...]
        gbuf[...] = nt(cot[...], wts[2])

    fm2 = arrive(2)
    with scope("dense1"):

        def dense_z(i, _):
            here = pl.ds(pl.multiple_of(i * blk, blk), blk)
            mean = ((fown[here, :] + nn(place[here, :], fm2)) * inv[here, :]).astype(BF16)
            mbuf[here, :] = mean
            z = zbuf[here, :] + nn(mean, wts[1])
            sig = 1.0 / (1.0 + jnp.exp(-z))
            hbuf[here, :] = (z * sig).astype(BF16)
            zbuf[here, :] = sig * (1.0 + z * (1.0 - sig))
            return 0

        lax.fori_loop(0, nodes // blk, dense_z, 0)
        wpart[pl.ds(2 * dim, dim), :] = tn(hbuf[...], cot[...])

    gm2 = arrive(3)
    with scope("dense2"):

        def dense_g(i, acc):
            here = pl.ds(pl.multiple_of(i * blk, blk), blk)
            gsum = (gown[here, :] + nn(place[here, :], gm2)).astype(BF16)
            gown[here, :] = gsum.astype(F32)
            gh = gbuf[here, :] + nt(gsum, wts[3])
            gz = (gh * zbuf[here, :]).astype(BF16)
            gzbuf[here, :] = gz
            gzf = gz.astype(F32)
            ybuf[here, :] = (gzf * inv[here, :]).astype(BF16)
            return acc + jnp.sum(gzf, axis=0, keepdims=True)

        bpart[...] = lax.fori_loop(0, nodes // blk, dense_g, jnp.zeros((1, dim), F32))

    with scope("pick3"):
        fill(4, tn(place[...], ybuf[...]))
    exchange(4)

    with scope("wgrad"):
        wpart[pl.ds(0, dim), :] = tn(feat[...], gzbuf[...])
        wpart[pl.ds(dim, dim), :] = tn(mbuf[...], gzbuf[...])
        wpart[pl.ds(3 * dim, dim), :] = tn(hbuf[...], gown[:nodes, :].astype(BF16))
    mine = pl.ds(pl.multiple_of(core * half, half), half)
    other = pl.ds(pl.multiple_of((1 - core) * half, half), half)
    pair_w = pltpu.make_async_remote_copy(
        src_ref=wpart.at[other, :],
        dst_ref=wpair,
        send_sem=ssem.at[6],
        recv_sem=rsem.at[6],
        device_id=partner,
        device_id_type=MESH,
    )
    pair_b = pltpu.make_async_remote_copy(
        src_ref=bpart,
        dst_ref=bpair,
        send_sem=ssem.at[7],
        recv_sem=rsem.at[7],
        device_id=partner,
        device_id_type=MESH,
    )
    pair_w.start()
    pair_b.start()

    with scope("own3"):
        hown[...] = tn(adj[:nodes, :], ybuf[...])

    with scope("pairwait"):
        pair_w.wait()
        pair_b.wait()
    rs_send[...] = (wpart[mine, :] + wpair[...]).astype(rs_send.dtype).reshape(rs_send.shape)
    bsum[...] = bpart[...] + bpair[...]

    def scatter(a, b):
        pltpu.make_async_remote_copy(
            src_ref=rs_send.at[lax.div(a * n_sub + b, 2)],
            dst_ref=rs_recv.at[chip],
            send_sem=ssem.at[8],
            recv_sem=rsem.at[8],
            device_id=(a, b),
            device_id_type=MESH,
        ).start()
        pltpu.make_async_remote_copy(
            src_ref=bsum,
            dst_ref=brecv.at[chip],
            send_sem=ssem.at[9],
            recv_sem=rsem.at[9],
            device_id=(a, b),
            device_id_type=MESH,
        ).start()

    with scope("scatter"):
        each(scatter, False)
        own_rs = pltpu.make_async_copy(rs_send.at[chip], rs_recv.at[chip], loc_sem.at[6])
        own_rs.start()
        own_b = pltpu.make_async_copy(bsum, brecv.at[chip], loc_sem.at[7])
        own_b.start()

    hm = arrive(4)
    fill(5, hown[nodes:, :] + tn(adj[nodes:, nodes:], hm))
    exchange(5)
    with scope("own4"):
        hown[:nodes, :] += tn(adj[nodes:, :nodes], hm)
        zbuf[...] = nt(gzbuf[...], wts[0])

    with scope("rswait"):
        own_rs.wait()
        own_b.wait()
        others = rs_recv.at[pl.ds(0, n_chip - 1)]
        pltpu.make_async_copy(others, others, rsem.at[8]).wait()
        others = brecv.at[pl.ds(0, n_chip - 1)]
        pltpu.make_async_copy(others, others, rsem.at[9]).wait()
    ag_send[...] = (jnp.sum(rs_recv[...].astype(F32), axis=0) * norm_factor).astype(ag_send.dtype)
    gb_ref[...] = jnp.sum(brecv[...], axis=0) * norm_factor

    def gather(a, b):
        pltpu.make_async_remote_copy(
            src_ref=ag_send,
            dst_ref=ag_all.at[core, chip],
            send_sem=ssem.at[10],
            recv_sem=rsem.at[10],
            device_id=(a, b),
            device_id_type=MESH,
        ).start()

    with scope("gather"):
        each(gather, False)
        own_ag = pltpu.make_async_copy(ag_send, ag_all.at[core, chip], loc_sem.at[8])
        own_ag.start()

    hm2 = arrive(5)
    with scope("last"):

        def last(i, _):
            here = pl.ds(pl.multiple_of(i * blk, blk), blk)
            hsum = (hown[here, :] + nn(place[here, :], hm2)).astype(BF16)
            gfeat_ref[here, :] = (zbuf[here, :] + nt(hsum, wts[1])).astype(BF16)
            return 0

        lax.fori_loop(0, nodes // blk, last, 0)

    with scope("agwait"):
        own_ag.wait()
        others = ag_all.at[core, pl.ds(0, n_chip - 1)]
        pltpu.make_async_copy(others, others, rsem.at[10]).wait()
    swap = pltpu.make_async_remote_copy(
        src_ref=ag_all.at[core],
        dst_ref=ag_all.at[core],
        send_sem=ssem.at[11],
        recv_sem=rsem.at[11],
        device_id=partner,
        device_id_type=MESH,
    )
    with scope("swap"):
        swap.start()
        swap.wait()
    gw_ref[...] = ag_all[...].astype(F32).reshape(4 * dim, dim)

    with scope("drain"):
        for k in range(6):
            sent(k)
        for ref, k in ((rs_send, 8), (brecv, 9)):
            others = ref.at[pl.ds(0, n_chip - 1)]
            pltpu.make_async_copy(others, others, ssem.at[k]).wait()
        others = ag_all.at[core, pl.ds(0, n_chip - 1)]
        pltpu.make_async_copy(others, others, ssem.at[10]).wait()


def shards(
    n_dom,
    n_sub,
    features,
    cotangent,
    w_self_one,
    w_nbr_one,
    bias_one,
    w_self_two,
    w_nbr_two,
    in_count,
    send_list,
    src_slot,
    dst_slot,
    edge_count,
):
    nodes, dim = features.shape
    n_dev = n_dom * n_sub
    n_chip = n_dev // 2
    per_peer = send_list.shape[2]
    n_mir = n_dev * per_peer
    slots = nodes + n_mir
    edges = src_slot.shape[1]
    own_rows = 2 * dim // n_chip
    vm = pl.BlockSpec(memory_space=pltpu.VMEM)
    hbm = pl.BlockSpec(memory_space=pltpu.HBM)
    norm_factor = float(nodes * n_dev) ** -0.5
    full = pltpu.VMEM((nodes, dim), F32)
    fullb = pltpu.VMEM((nodes, dim), BF16)
    allf = pltpu.VMEM((slots, dim), F32)
    msgs = pltpu.VMEM((6, n_dev, per_peer, dim), BF16)
    rs_t = BF16
    ag_t = BF16
    gfeat, gw, gb = pl.pallas_call(
        functools.partial(kernel, n_dom, n_sub, norm_factor),
        out_shape=(
            jax.ShapeDtypeStruct((nodes, dim), BF16),
            jax.ShapeDtypeStruct((4 * dim, dim), F32),
            jax.ShapeDtypeStruct((1, dim), F32),
        ),
        in_specs=[hbm] * 12,
        out_specs=(vm, vm, vm),
        scratch_shapes=[
            pltpu.VMEM((1, 1), jnp.int32),
            pltpu.VMEM((1, edges), jnp.int32),
            pltpu.VMEM((1, edges), jnp.int32),
            pltpu.VMEM((per_peer, n_dev), jnp.int32),
            pltpu.VMEM((1, nodes), jnp.int32),
            pltpu.VMEM((1, dim), F32),
            fullb,
            fullb,
            pltpu.VMEM((4, dim, dim), BF16),
            pltpu.VMEM((slots, edges), ONE_HOT),
            pltpu.VMEM((slots, edges), ONE_HOT),
            pltpu.VMEM((slots, slots), BF16),
            pltpu.VMEM((nodes, n_mir), BF16),
            full,
            fullb,
            full,
            full,
            allf,
            allf,
            allf,
            fullb,
            fullb,
            fullb,
            msgs,
            msgs,
            pltpu.VMEM((4 * dim, dim), F32),
            pltpu.VMEM((1, dim), F32),
            pltpu.VMEM((2 * dim, dim), F32),
            pltpu.VMEM((1, dim), F32),
            pltpu.VMEM((1, dim), F32),
            pltpu.VMEM((n_chip, 1, dim), F32),
            pltpu.VMEM((n_chip, own_rows, dim), rs_t),
            pltpu.VMEM((n_chip, own_rows, dim), rs_t),
            pltpu.VMEM((own_rows, dim), ag_t),
            pltpu.VMEM((2, n_chip, own_rows, dim), ag_t),
            pltpu.SemaphoreType.DMA((12,)),
            pltpu.SemaphoreType.DMA((9,)),
            pltpu.SemaphoreType.DMA((12,)),
            pltpu.SemaphoreType.DMA((12,)),
        ],
        compiler_params=pltpu.CompilerParams(
            collective_id=0, has_side_effects=True, vmem_limit_bytes=44 << 20
        ),
    )(
        edge_count.reshape(1, 1),
        *(
            pltpu.with_memory_space_constraint(x, pltpu.HBM)
            for x in (
                src_slot,
                dst_slot,
                send_list[0].T,
                in_count.reshape(1, nodes),
                bias_one.reshape(1, dim),
                features,
                cotangent,
                w_self_one,
                w_nbr_one,
                w_self_two,
                w_nbr_two,
            )
        ),
    )
    return gfeat, gw.reshape(4, dim, dim), gb.reshape(dim)


def solution(mesh):
    both = ("dom", "sub")
    return jax.shard_map(
        functools.partial(shards, mesh.shape["dom"], mesh.shape["sub"]),
        mesh=mesh,
        in_specs=(
            P(both, None),
            P(both, None),
            P(),
            P(),
            P(),
            P(),
            P(),
            P(both),
            P(both, None, None),
            P(both, None),
            P(both, None),
            P(both),
        ),
        out_specs=(P(both, None), P(), P()),
        check_vma=False,
    )
```

```python
import contextlib
import functools

import jax
import jax.numpy as jnp
from jax import lax
from jax.experimental import pallas as pl
from jax.experimental.pallas import tpu as pltpu
from jax.sharding import PartitionSpec as P

MESH = pl.DeviceIdType.MESH
F32 = jnp.float32
BF16 = jnp.bfloat16
ONE_HOT = jnp.float8_e4m3fn
FAR = (10, 9, 11, 6, 14, 8, 2, 5, 7, 13, 15, 4, 12, 1, 3)


def scope(name):
    return contextlib.nullcontext()


def nn(left, right):
    return jnp.dot(left, right, preferred_element_type=F32)


def tn(left, right):
    return lax.dot_general(left, right, (((0,), (0,)), ((), ())), preferred_element_type=F32)


def nt(left, right):
    return lax.dot_general(left, right, (((1,), (1,)), ((), ())), preferred_element_type=F32)


def digits(codes):
    total = 0
    for code in reversed(codes):
        total = total * 16 + code
    return total


def wrap4(v):
    return jnp.where(v >= 4, v - 4, v)


def kernel(
    n_dom,
    n_sub,
    norm_factor,
    count_hbm,
    src_hbm,
    dst_hbm,
    send_hbm,
    in_count_hbm,
    bias_hbm,
    feat_hbm,
    cot_hbm,
    ws1_hbm,
    wn1_hbm,
    ws2_hbm,
    wn2_hbm,
    gfeat_ref,
    gw_ref,
    gb_ref,
    count_ref,
    src_ref,
    dst_ref,
    send_ref,
    in_count_ref,
    bias_ref,
    feat,
    cot,
    wts,
    src_hot,
    dst_hot,
    adj,
    place,
    inv,
    ybuf,
    zbuf,
    gbuf,
    fown,
    gown,
    hown,
    mbuf,
    hbuf,
    gzbuf,
    gsbuf,
    sends,
    recvs,
    wpart,
    bpart,
    wpair,
    bpair,
    bsum,
    brecv,
    rs_send,
    rs_recv,
    ag_send,
    ag_all,
    in_sem,
    loc_sem,
    ssem,
    rsem,
):
    nodes, dim = feat.shape
    n_dev = n_dom * n_sub
    n_chip = n_dev // 2
    n_mir = place.shape[1]
    slots = nodes + n_mir
    per_peer = n_mir // n_dev
    half = wpair.shape[0]
    blk = 256
    d = lax.axis_index("dom")
    s = lax.axis_index("sub")
    me = d * n_sub + s
    chip = lax.div(me, 2)
    core = lax.rem(me, 2)
    at_y, at_z, at_x = lax.div(d, 4), lax.rem(d, 4), lax.div(s, 2)
    partner = (d, s + 1 - 2 * core)

    small = [
        (send_hbm, send_ref),
        (in_count_hbm, in_count_ref),
        (count_hbm, count_ref),
        (src_hbm, src_ref),
        (dst_hbm, dst_ref),
        (bias_hbm, bias_ref),
    ]
    large = [
        (feat_hbm, feat),
        (cot_hbm, cot),
        (ws1_hbm, wts.at[0]),
        (wn1_hbm, wts.at[1]),
        (ws2_hbm, wts.at[2]),
        (wn2_hbm, wts.at[3]),
    ]
    loads = [
        pltpu.make_async_copy(a, b, in_sem.at[i]) for i, (a, b) in enumerate(small + large)
    ]
    for c in loads:
        c.start()

    xs = [wrap4(at_x + k) * 2 for k in (2, 1, 3, 0)]
    cores = [1 - core, core]

    def each(do, both):
        def line(dom, is_mine):
            for k in range(4):
                for j in range(2):
                    if (both or j == 1) and not (is_mine and k == 3 and j == 1):
                        do(dom, xs[k] + cores[j])

        def dom_of(code):
            return wrap4(at_y + lax.div(code, 4)) * 4 + wrap4(at_z + lax.rem(code, 4))

        def turn(_, left):
            line(dom_of(lax.rem(left, 16)), False)
            return lax.div(left, 16)

        lax.fori_loop(0, 7, turn, jnp.int32(digits(FAR[:7])))
        lax.fori_loop(0, 7, turn, jnp.int32(digits(FAR[7:14])))
        line(dom_of(jnp.int32(FAR[14])), False)
        line(d, True)

    barrier = pltpu.get_barrier_semaphore()
    with scope("greet"):
        each(
            lambda a, b: pl.semaphore_signal(barrier, 1, device_id=(a, b), device_id_type=MESH),
            True,
        )

    def exchange(k):
        def one(a, b):
            pltpu.make_async_remote_copy(
                src_ref=sends.at[k, a * n_sub + b],
                dst_ref=recvs.at[k, me],
                send_sem=ssem.at[k],
                recv_sem=rsem.at[k],
                device_id=(a, b),
                device_id_type=MESH,
            ).start()

        with scope(f"ex{k}"):
            each(one, True)
            pltpu.make_async_copy(sends.at[k, me], recvs.at[k, me], loc_sem.at[k]).start()

    def arrive(k):
        with scope(f"arr{k}"):
            pltpu.make_async_copy(sends.at[k, me], recvs.at[k, me], loc_sem.at[k]).wait()
            all_in = recvs.at[k, pl.ds(0, n_dev - 1)]
            pltpu.make_async_copy(all_in, all_in, rsem.at[k]).wait()
        return recvs[k].reshape(n_mir, dim)

    def sent(k):
        all_out = sends.at[k, pl.ds(0, n_dev - 1)]
        pltpu.make_async_copy(all_out, all_out, ssem.at[k]).wait()

    def rows(ref, i):
        return ref.at[pl.ds(pl.multiple_of(i * blk, blk), blk), :]

    def fill(k, value):
        sends[k] = value.astype(BF16).reshape(n_dev, per_peer, dim)

    def hot_block(index_row, i):
        shape = (blk, index_row.shape[1])
        ids = lax.broadcasted_iota(jnp.int32, shape, 0).astype(F32).astype(BF16)
        here = (index_row - i * blk).astype(F32).astype(BF16)
        return jnp.where(ids == here, jnp.ones(shape, BF16), jnp.zeros(shape, BF16))

    with scope("prepf"):
        loads[0].wait()
        lists = send_ref[...]
        parts = jnp.concatenate([lists // 32, lists % 32], axis=0).astype(F32).astype(BF16)
        lane = lax.broadcasted_iota(jnp.int32, (n_dev, n_mir), 1)
        widen = (
            lax.shift_right_logical(lane, 2) == lax.broadcasted_iota(jnp.int32, (n_dev, n_mir), 0)
        ).astype(BF16)
        wide = nn(parts, widen)
        wide = wide[:per_peer] * 32.0 + wide[per_peer:]
        turn_of = lax.broadcasted_iota(jnp.int32, (per_peer, n_mir), 1) & 3
        mine_of = turn_of == lax.broadcasted_iota(jnp.int32, (per_peer, n_mir), 0)
        picked = jnp.sum(jnp.where(mine_of, wide, 0.0), axis=0, keepdims=True).astype(jnp.int32)
        for i in range(nodes // blk):
            place[pl.ds(i * blk, blk), :] = hot_block(picked, i)
        loads[6].wait()
        fill(0, tn(place[...], feat[...]))

    with scope("bwait"):
        pl.semaphore_wait(barrier, n_dev - 1)
    exchange(0)

    with scope("prepg"):
        loads[1].wait()
        inv_row = 1.0 / jnp.maximum(in_count_ref[...], 1).astype(F32)
        inv_col = jnp.broadcast_to(inv_row, (128, nodes)).T
        inv[...] = jnp.concatenate([inv_col] * (dim // 128), axis=1)
        loads[7].wait()
        ybuf[...] = (cot[...].astype(F32) * inv[...]).astype(BF16)
        fill(1, tn(place[...], ybuf[...]))
    exchange(1)

    with scope("hot"):
        for c in loads[2:6]:
            c.wait()
        edges = src_ref.shape[1]
        live = lax.broadcasted_iota(jnp.int32, (1, edges), 1) < count_ref[...]
        src_row = jnp.where(live, src_ref[...], -1)
        dst_row = jnp.where(live, dst_ref[...], -1)

        def hot(i, _):
            rows(src_hot, i)[...] = hot_block(src_row, i).astype(ONE_HOT)
            rows(dst_hot, i)[...] = hot_block(dst_row, i).astype(ONE_HOT)
            return 0

        lax.fori_loop(0, slots // blk, hot, 0)

    masters = nodes // blk
    with scope("buildm"):

        def build_rows(i, _):
            rows(adj, i)[...] = nt(rows(dst_hot, i)[...], src_hot[...]).astype(BF16)
            return 0

        lax.fori_loop(masters, slots // blk, build_rows, 0)

        def build_columns(i, _):
            here = pl.ds(pl.multiple_of(i * blk, blk), blk)
            adj[here, nodes:] = nt(dst_hot[here, :], src_hot[nodes:, :]).astype(BF16)
            return 0

        lax.fori_loop(0, masters, build_columns, 0)

    with scope("own1"):
        fown[nodes:, :] = nn(adj[nodes:, :nodes], feat[...])
        gown[nodes:, :] = tn(adj[:nodes, nodes:], ybuf[...])
        for c in loads[8:]:
            c.wait()
        zbuf[...] = nn(feat[...], wts[0]) + bias_ref[...]
        gbuf[...] = nt(cot[...], wts[2])

    fm = arrive(0)
    fill(2, fown[nodes:, :] + nn(adj[nodes:, nodes:], fm))
    exchange(2)
    gm = arrive(1)
    fill(3, gown[nodes:, :] + tn(adj[nodes:, nodes:], gm))
    exchange(3)

    with scope("buildo"):

        def build_rest(i, _):
            here = pl.ds(pl.multiple_of(i * blk, blk), blk)
            adj[here, :nodes] = nt(dst_hot[here, :], src_hot[:nodes, :]).astype(BF16)
            return 0

        lax.fori_loop(0, masters, build_rest, 0)
    with scope("own2"):
        fown[:nodes, :] = nn(adj[:nodes, :nodes], feat[...]) + nn(adj[:nodes, nodes:], fm)
        gown[:nodes, :] = tn(adj[:nodes, :nodes], ybuf[...]) + tn(adj[nodes:, :nodes], gm)

    big = nodes // 2
    fm2 = arrive(2)
    with scope("dense1"):
        for i in range(nodes // big):
            here = pl.ds(i * big, big)
            mean = ((fown[here, :] + nn(place[here, :], fm2)) * inv[here, :]).astype(BF16)
            mbuf[here, :] = mean
            z = zbuf[here, :] + nn(mean, wts[1])
            sig = 1.0 / (1.0 + jnp.exp(-z))
            hbuf[here, :] = (z * sig).astype(BF16)
            zbuf[here, :] = sig * (1.0 + z * (1.0 - sig))
        wpart[pl.ds(2 * dim, dim), :] = tn(hbuf[...], cot[...])

    gm2 = arrive(3)
    with scope("dense2"):
        bias_sum = jnp.zeros((1, dim), F32)
        for i in range(nodes // big):
            here = pl.ds(i * big, big)
            gsum = (gown[here, :] + nn(place[here, :], gm2)).astype(BF16)
            gsbuf[here, :] = gsum
            gh = gbuf[here, :] + nt(gsum, wts[3])
            gz = (gh * zbuf[here, :]).astype(BF16)
            gzbuf[here, :] = gz
            gzf = gz.astype(F32)
            ybuf[here, :] = (gzf * inv[here, :]).astype(BF16)
            bias_sum += jnp.sum(gzf, axis=0, keepdims=True)
        bpart[...] = bias_sum

    with scope("wgrad"):
        wpart[pl.ds(0, dim), :] = tn(feat[...], gzbuf[...])
        wpart[pl.ds(dim, dim), :] = tn(mbuf[...], gzbuf[...])
        wpart[pl.ds(3 * dim, dim), :] = tn(hbuf[...], gsbuf[...])
    mine = pl.ds(pl.multiple_of(core * half, half), half)
    other = pl.ds(pl.multiple_of((1 - core) * half, half), half)
    pair_w = pltpu.make_async_remote_copy(
        src_ref=wpart.at[other, :],
        dst_ref=wpair,
        send_sem=ssem.at[6],
        recv_sem=rsem.at[6],
        device_id=partner,
        device_id_type=MESH,
    )
    pair_b = pltpu.make_async_remote_copy(
        src_ref=bpart,
        dst_ref=bpair,
        send_sem=ssem.at[7],
        recv_sem=rsem.at[7],
        device_id=partner,
        device_id_type=MESH,
    )
    pair_w.start()
    pair_b.start()

    with scope("pick3"):
        fill(4, tn(place[...], ybuf[...]))
    exchange(4)

    with scope("own3"):
        hown[...] = tn(adj[:nodes, :], ybuf[...])

    with scope("pairwait"):
        pair_w.wait()
        pair_b.wait()
    rs_send[...] = (wpart[mine, :] + wpair[...]).astype(rs_send.dtype).reshape(rs_send.shape)
    bsum[...] = bpart[...] + bpair[...]

    def scatter(a, b):
        pltpu.make_async_remote_copy(
            src_ref=rs_send.at[lax.div(a * n_sub + b, 2)],
            dst_ref=rs_recv.at[chip],
            send_sem=ssem.at[8],
            recv_sem=rsem.at[8],
            device_id=(a, b),
            device_id_type=MESH,
        ).start()
        pltpu.make_async_remote_copy(
            src_ref=bsum,
            dst_ref=brecv.at[chip],
            send_sem=ssem.at[9],
            recv_sem=rsem.at[9],
            device_id=(a, b),
            device_id_type=MESH,
        ).start()

    with scope("scatter"):
        each(scatter, False)
        own_rs = pltpu.make_async_copy(rs_send.at[chip], rs_recv.at[chip], loc_sem.at[6])
        own_rs.start()
        own_b = pltpu.make_async_copy(bsum, brecv.at[chip], loc_sem.at[7])
        own_b.start()

    hm = arrive(4)
    fill(5, hown[nodes:, :] + tn(adj[nodes:, nodes:], hm))
    exchange(5)
    with scope("own4"):
        hown[:nodes, :] += tn(adj[nodes:, :nodes], hm)
        zbuf[...] = nt(gzbuf[...], wts[0])

    with scope("rswait"):
        own_rs.wait()
        own_b.wait()
        others = rs_recv.at[pl.ds(0, n_chip - 1)]
        pltpu.make_async_copy(others, others, rsem.at[8]).wait()
        others = brecv.at[pl.ds(0, n_chip - 1)]
        pltpu.make_async_copy(others, others, rsem.at[9]).wait()
    ag_send[...] = (jnp.sum(rs_recv[...].astype(F32), axis=0) * norm_factor).astype(ag_send.dtype)
    gb_ref[...] = jnp.sum(brecv[...], axis=0) * norm_factor

    def gather(a, b):
        pltpu.make_async_remote_copy(
            src_ref=ag_send,
            dst_ref=ag_all.at[core, chip],
            send_sem=ssem.at[10],
            recv_sem=rsem.at[10],
            device_id=(a, b),
            device_id_type=MESH,
        ).start()

    with scope("gather"):
        each(gather, False)
        own_ag = pltpu.make_async_copy(ag_send, ag_all.at[core, chip], loc_sem.at[8])
        own_ag.start()

    hm2 = arrive(5)
    with scope("last"):

        for i in range(nodes // big):
            here = pl.ds(i * big, big)
            hsum = (hown[here, :] + nn(place[here, :], hm2)).astype(BF16)
            gfeat_ref[here, :] = (zbuf[here, :] + nt(hsum, wts[1])).astype(BF16)

    with scope("agwait"):
        own_ag.wait()
        others = ag_all.at[core, pl.ds(0, n_chip - 1)]
        pltpu.make_async_copy(others, others, rsem.at[10]).wait()
    swap = pltpu.make_async_remote_copy(
        src_ref=ag_all.at[core],
        dst_ref=ag_all.at[core],
        send_sem=ssem.at[11],
        recv_sem=rsem.at[11],
        device_id=partner,
        device_id_type=MESH,
    )
    with scope("swap"):
        swap.start()
        swap.wait()
    gw_ref[...] = ag_all[...].astype(F32).reshape(4 * dim, dim)

    with scope("drain"):
        for k in range(6):
            sent(k)
        for ref, k in ((rs_send, 8), (brecv, 9)):
            others = ref.at[pl.ds(0, n_chip - 1)]
            pltpu.make_async_copy(others, others, ssem.at[k]).wait()
        others = ag_all.at[core, pl.ds(0, n_chip - 1)]
        pltpu.make_async_copy(others, others, ssem.at[10]).wait()


def put(*refs):
    sem = refs[-1]
    half = len(refs) // 2
    copies = [
        pltpu.make_async_copy(a, b, sem.at[i])
        for i, (a, b) in enumerate(zip(refs[:half], refs[half:-1]))
    ]
    for c in copies:
        c.start()
    for c in copies:
        c.wait()


def shards(
    n_dom,
    n_sub,
    features,
    cotangent,
    w_self_one,
    w_nbr_one,
    bias_one,
    w_self_two,
    w_nbr_two,
    in_count,
    send_list,
    src_slot,
    dst_slot,
    edge_count,
):
    nodes, dim = features.shape
    n_dev = n_dom * n_sub
    n_chip = n_dev // 2
    per_peer = send_list.shape[2]
    n_mir = n_dev * per_peer
    slots = nodes + n_mir
    edges = src_slot.shape[1]
    own_rows = 2 * dim // n_chip
    vm = pl.BlockSpec(memory_space=pltpu.VMEM)
    hbm = pl.BlockSpec(memory_space=pltpu.HBM)
    norm_factor = float(nodes * n_dev) ** -0.5
    full = pltpu.VMEM((nodes, dim), F32)
    fullb = pltpu.VMEM((nodes, dim), BF16)
    allf = pltpu.VMEM((slots, dim), F32)
    msgs = pltpu.VMEM((6, n_dev, per_peer, dim), BF16)
    rs_t = BF16
    ag_t = BF16
    gfeat, gw, gb = pl.pallas_call(
        functools.partial(kernel, n_dom, n_sub, norm_factor),
        out_shape=(
            jax.ShapeDtypeStruct((nodes, dim), BF16),
            jax.ShapeDtypeStruct((4 * dim, dim), F32),
            jax.ShapeDtypeStruct((1, dim), F32),
        ),
        in_specs=[hbm] * 12,
        out_specs=(vm, vm, vm),
        scratch_shapes=[
            pltpu.VMEM((1, 1), jnp.int32),
            pltpu.VMEM((1, edges), jnp.int32),
            pltpu.VMEM((1, edges), jnp.int32),
            pltpu.VMEM((per_peer, n_dev), jnp.int32),
            pltpu.VMEM((1, nodes), jnp.int32),
            pltpu.VMEM((1, dim), F32),
            fullb,
            fullb,
            pltpu.VMEM((4, dim, dim), BF16),
            pltpu.VMEM((slots, edges), ONE_HOT),
            pltpu.VMEM((slots, edges), ONE_HOT),
            pltpu.VMEM((slots, slots), BF16),
            pltpu.VMEM((nodes, n_mir), BF16),
            full,
            fullb,
            full,
            full,
            allf,
            allf,
            allf,
            fullb,
            fullb,
            fullb,
            fullb,
            msgs,
            msgs,
            pltpu.VMEM((4 * dim, dim), F32),
            pltpu.VMEM((1, dim), F32),
            pltpu.VMEM((2 * dim, dim), F32),
            pltpu.VMEM((1, dim), F32),
            pltpu.VMEM((1, dim), F32),
            pltpu.VMEM((n_chip, 1, dim), F32),
            pltpu.VMEM((n_chip, own_rows, dim), rs_t),
            pltpu.VMEM((n_chip, own_rows, dim), rs_t),
            pltpu.VMEM((own_rows, dim), ag_t),
            pltpu.VMEM((2, n_chip, own_rows, dim), ag_t),
            pltpu.SemaphoreType.DMA((12,)),
            pltpu.SemaphoreType.DMA((9,)),
            pltpu.SemaphoreType.DMA((12,)),
            pltpu.SemaphoreType.DMA((12,)),
        ],
        compiler_params=pltpu.CompilerParams(
            collective_id=0, has_side_effects=True, vmem_limit_bytes=44 << 20
        ),
    )(
        edge_count.reshape(1, 1),
        *(
            pltpu.with_memory_space_constraint(x, pltpu.HBM)
            for x in (
                src_slot,
                dst_slot,
                send_list[0].T,
                in_count.reshape(1, nodes),
                bias_one.reshape(1, dim),
                features,
                cotangent,
                w_self_one,
                w_nbr_one,
                w_self_two,
                w_nbr_two,
            )
        ),
    )
    results = (gfeat, gw, gb)
    gfeat, gw, gb = pl.pallas_call(
        put,
        out_shape=tuple(jax.ShapeDtypeStruct(x.shape, x.dtype) for x in results),
        in_specs=[vm] * 3,
        out_specs=(hbm,) * 3,
        scratch_shapes=[pltpu.SemaphoreType.DMA((3,))],
        compiler_params=pltpu.CompilerParams(vmem_limit_bytes=1 << 20),
    )(*results)
    return gfeat, gw.reshape(4, dim, dim), gb.reshape(dim)


def solution(mesh):
    both = ("dom", "sub")
    return jax.shard_map(
        functools.partial(shards, mesh.shape["dom"], mesh.shape["sub"]),
        mesh=mesh,
        in_specs=(
            P(both, None),
            P(both, None),
            P(),
            P(),
            P(),
            P(),
            P(),
            P(both),
            P(both, None, None),
            P(both, None),
            P(both, None),
            P(both),
        ),
        out_specs=(P(both, None), P(), P()),
        check_vma=False,
    )
```

```python
import contextlib
import functools

import jax
import jax.numpy as jnp
from jax import lax
from jax.experimental import pallas as pl
from jax.experimental.pallas import tpu as pltpu
from jax.sharding import PartitionSpec as P

MESH = pl.DeviceIdType.MESH
F32 = jnp.float32
BF16 = jnp.bfloat16
ONE_HOT = jnp.float8_e4m3fn
FAR = (10, 9, 11, 6, 14, 8, 2, 5, 7, 13, 15, 4, 12, 1, 3)


def scope(name):
    return contextlib.nullcontext()


def nn(left, right):
    return jnp.dot(left, right, preferred_element_type=F32)


def tn(left, right):
    return lax.dot_general(left, right, (((0,), (0,)), ((), ())), preferred_element_type=F32)


def nt(left, right):
    return lax.dot_general(left, right, (((1,), (1,)), ((), ())), preferred_element_type=F32)


def digits(codes):
    total = 0
    for code in reversed(codes):
        total = total * 16 + code
    return total


def wrap4(v):
    return jnp.where(v >= 4, v - 4, v)


def kernel(
    n_dom,
    n_sub,
    norm_factor,
    count_hbm,
    src_hbm,
    dst_hbm,
    send_hbm,
    in_count_hbm,
    bias_hbm,
    feat_hbm,
    cot_hbm,
    ws1_hbm,
    wn1_hbm,
    ws2_hbm,
    wn2_hbm,
    gfeat_ref,
    gw_ref,
    gb_ref,
    count_ref,
    src_ref,
    dst_ref,
    send_ref,
    in_count_ref,
    bias_ref,
    feat,
    cot,
    wts,
    src_hot,
    dst_hot,
    adj,
    place,
    picks,
    inv,
    ybuf,
    zbuf,
    gbuf,
    fown,
    gown,
    hown,
    mbuf,
    hbuf,
    gzbuf,
    gsbuf,
    sends,
    recvs,
    wpart,
    bpart,
    wsend,
    wpair,
    bpair,
    bsum,
    brecv,
    rs_send,
    rs_recv,
    ag_send,
    ag_all,
    in_sem,
    loc_sem,
    ssem,
    rsem,
):
    nodes, dim = feat.shape
    n_dev = n_dom * n_sub
    n_chip = n_dev // 2
    n_mir = place.shape[1]
    slots = nodes + n_mir
    per_peer = n_mir // n_dev
    half = wpair.shape[0]
    blk = 256
    d = lax.axis_index("dom")
    s = lax.axis_index("sub")
    me = d * n_sub + s
    chip = lax.div(me, 2)
    core = lax.rem(me, 2)
    at_y, at_z, at_x = lax.div(d, 4), lax.rem(d, 4), lax.div(s, 2)
    partner = (d, s + 1 - 2 * core)

    small = [
        (send_hbm, send_ref),
        (in_count_hbm, in_count_ref),
        (count_hbm, count_ref),
        (src_hbm, src_ref),
        (dst_hbm, dst_ref),
        (bias_hbm, bias_ref),
    ]
    large = [
        (feat_hbm, feat),
        (cot_hbm, cot),
        (ws1_hbm, wts.at[0]),
        (wn1_hbm, wts.at[1]),
        (ws2_hbm, wts.at[2]),
        (wn2_hbm, wts.at[3]),
    ]
    loads = [
        pltpu.make_async_copy(a, b, in_sem.at[i]) for i, (a, b) in enumerate(small + large)
    ]
    for c in loads:
        c.start()

    xs = [wrap4(at_x + k) * 2 for k in (2, 1, 3, 0)]
    cores = [1 - core, core]

    def each(do, both):
        def line(dom, is_mine):
            for k in range(4):
                for j in range(2):
                    if (both or j == 1) and not (is_mine and k == 3 and j == 1):
                        do(dom, xs[k] + cores[j])

        def dom_of(code):
            return wrap4(at_y + lax.div(code, 4)) * 4 + wrap4(at_z + lax.rem(code, 4))

        def turn(_, left):
            line(dom_of(lax.rem(left, 16)), False)
            return lax.div(left, 16)

        lax.fori_loop(0, 7, turn, jnp.int32(digits(FAR[:7])))
        lax.fori_loop(0, 7, turn, jnp.int32(digits(FAR[7:14])))
        line(dom_of(jnp.int32(FAR[14])), False)
        line(d, True)

    barrier = pltpu.get_barrier_semaphore()
    with scope("greet"):
        each(
            lambda a, b: pl.semaphore_signal(barrier, 1, device_id=(a, b), device_id_type=MESH),
            True,
        )

    def exchange(k):
        def one(a, b):
            pltpu.make_async_remote_copy(
                src_ref=sends.at[k, a * n_sub + b],
                dst_ref=recvs.at[k, me],
                send_sem=ssem.at[k],
                recv_sem=rsem.at[k],
                device_id=(a, b),
                device_id_type=MESH,
            ).start()

        with scope(f"ex{k}"):
            each(one, True)
            pltpu.make_async_copy(sends.at[k, me], recvs.at[k, me], loc_sem.at[k]).start()

    def arrive(k):
        with scope(f"arr{k}"):
            pltpu.make_async_copy(sends.at[k, me], recvs.at[k, me], loc_sem.at[k]).wait()
            all_in = recvs.at[k, pl.ds(0, n_dev - 1)]
            pltpu.make_async_copy(all_in, all_in, rsem.at[k]).wait()
        return recvs[k].reshape(n_mir, dim)

    def sent(k):
        all_out = sends.at[k, pl.ds(0, n_dev - 1)]
        pltpu.make_async_copy(all_out, all_out, ssem.at[k]).wait()

    def rows(ref, i):
        return ref.at[pl.ds(pl.multiple_of(i * blk, blk), blk), :]

    def fill(k, value):
        sends[k] = value.astype(BF16).reshape(n_dev, per_peer, dim)

    def hot_block(index_row, i):
        shape = (blk, index_row.shape[1])
        ids = lax.broadcasted_iota(jnp.int32, shape, 0).astype(F32).astype(BF16)
        here = (index_row - i * blk).astype(F32).astype(BF16)
        return jnp.where(ids == here, jnp.ones(shape, BF16), jnp.zeros(shape, BF16))

    with scope("prepf"):
        loads[0].wait()
        lists = send_ref[...]
        parts = jnp.concatenate([lists // 32, lists % 32], axis=0).astype(F32).astype(BF16)
        lane = lax.broadcasted_iota(jnp.int32, (n_dev, n_mir), 1)
        widen = (
            lax.shift_right_logical(lane, 2) == lax.broadcasted_iota(jnp.int32, (n_dev, n_mir), 0)
        ).astype(BF16)
        wide = nn(parts, widen)
        wide = wide[:per_peer] * 32.0 + wide[per_peer:]
        turn_of = lax.broadcasted_iota(jnp.int32, (per_peer, n_mir), 1) & 3
        mine_of = turn_of == lax.broadcasted_iota(jnp.int32, (per_peer, n_mir), 0)
        picked = jnp.sum(jnp.where(mine_of, wide, 0.0), axis=0, keepdims=True).astype(jnp.int32)
        for i in range(nodes // blk):
            place[pl.ds(i * blk, blk), :] = hot_block(picked, i)
        picks[...] = place[...].T
        loads[6].wait()
        fill(0, nn(picks[...], feat[...]))

    with scope("hot"):
        for c in loads[2:6]:
            c.wait()
        edges = src_ref.shape[1]
        live = lax.broadcasted_iota(jnp.int32, (1, edges), 1) < count_ref[...]
        src_row = jnp.where(live, src_ref[...], -1)
        dst_row = jnp.where(live, dst_ref[...], -1)

        def hot(i, _):
            rows(src_hot, i)[...] = hot_block(src_row, i).astype(ONE_HOT)
            rows(dst_hot, i)[...] = hot_block(dst_row, i).astype(ONE_HOT)
            return 0

        lax.fori_loop(0, slots // blk, hot, 0)

    with scope("bwait"):
        pl.semaphore_wait(barrier, n_dev - 1)
    exchange(0)

    with scope("prepg"):
        loads[1].wait()
        inv_row = 1.0 / jnp.maximum(in_count_ref[...], 1).astype(F32)
        inv_col = jnp.broadcast_to(inv_row, (128, nodes)).T
        inv[...] = jnp.concatenate([inv_col] * (dim // 128), axis=1)
        loads[7].wait()
        ybuf[...] = (cot[...].astype(F32) * inv[...]).astype(BF16)
        fill(1, nn(picks[...], ybuf[...]))
    exchange(1)

    masters = nodes // blk
    with scope("buildm"):

        def build_rows(i, _):
            rows(adj, i)[...] = nt(rows(dst_hot, i)[...], src_hot[...]).astype(BF16)
            return 0

        lax.fori_loop(masters, slots // blk, build_rows, 0)

        def build_columns(i, _):
            here = pl.ds(pl.multiple_of(i * blk, blk), blk)
            adj[here, nodes:] = nt(dst_hot[here, :], src_hot[nodes:, :]).astype(BF16)
            return 0

        lax.fori_loop(0, masters, build_columns, 0)

    with scope("own1"):
        fown[nodes:, :] = nn(adj[nodes:, :nodes], feat[...])
        gown[nodes:, :] = tn(adj[:nodes, nodes:], ybuf[...])
        for c in loads[8:]:
            c.wait()
        zbuf[...] = nn(feat[...], wts[0]) + bias_ref[...]
        gbuf[...] = nt(cot[...], wts[2])

    fm = arrive(0)
    fill(2, fown[nodes:, :] + nn(adj[nodes:, nodes:], fm))
    exchange(2)
    gm = arrive(1)
    fill(3, gown[nodes:, :] + tn(adj[nodes:, nodes:], gm))
    exchange(3)

    with scope("buildo"):

        def build_rest(i, _):
            here = pl.ds(pl.multiple_of(i * blk, blk), blk)
            adj[here, :nodes] = nt(dst_hot[here, :], src_hot[:nodes, :]).astype(BF16)
            return 0

        lax.fori_loop(0, masters, build_rest, 0)
    with scope("own2"):
        fown[:nodes, :] = nn(adj[:nodes, :nodes], feat[...]) + nn(adj[:nodes, nodes:], fm)
        gown[:nodes, :] = tn(adj[:nodes, :nodes], ybuf[...]) + tn(adj[nodes:, :nodes], gm)

    big = nodes // 2
    fm2 = arrive(2)
    with scope("dense1"):
        for i in range(nodes // big):
            here = pl.ds(i * big, big)
            mean = ((fown[here, :] + nn(place[here, :], fm2)) * inv[here, :]).astype(BF16)
            mbuf[here, :] = mean
            z = zbuf[here, :] + nn(mean, wts[1])
            sig = 1.0 / (1.0 + jnp.exp(-z))
            hbuf[here, :] = (z * sig).astype(BF16)
            zbuf[here, :] = sig * (1.0 + z * (1.0 - sig))
        wpart[pl.ds(2 * dim, dim), :] = tn(hbuf[...], cot[...])

    gm2 = arrive(3)
    with scope("dense2"):
        bias_sum = jnp.zeros((1, dim), F32)
        for i in range(nodes // big):
            here = pl.ds(i * big, big)
            gsum = (gown[here, :] + nn(place[here, :], gm2)).astype(BF16)
            gsbuf[here, :] = gsum
            gh = gbuf[here, :] + nt(gsum, wts[3])
            gz = (gh * zbuf[here, :]).astype(BF16)
            gzbuf[here, :] = gz
            gzf = gz.astype(F32)
            ybuf[here, :] = (gzf * inv[here, :]).astype(BF16)
            bias_sum += jnp.sum(gzf, axis=0, keepdims=True)
        bpart[...] = bias_sum

    with scope("pick3"):
        fill(4, nn(picks[...], ybuf[...]))
    exchange(4)

    with scope("wgrad"):
        wpart[pl.ds(0, dim), :] = tn(feat[...], gzbuf[...])
        wpart[pl.ds(dim, dim), :] = tn(mbuf[...], gzbuf[...])
        wpart[pl.ds(3 * dim, dim), :] = tn(hbuf[...], gsbuf[...])
    mine = pl.ds(pl.multiple_of(core * half, half), half)
    other = pl.ds(pl.multiple_of((1 - core) * half, half), half)
    wsend[...] = wpart[other, :].astype(BF16)
    pair_w = pltpu.make_async_remote_copy(
        src_ref=wsend,
        dst_ref=wpair,
        send_sem=ssem.at[6],
        recv_sem=rsem.at[6],
        device_id=partner,
        device_id_type=MESH,
    )
    pair_b = pltpu.make_async_remote_copy(
        src_ref=bpart,
        dst_ref=bpair,
        send_sem=ssem.at[7],
        recv_sem=rsem.at[7],
        device_id=partner,
        device_id_type=MESH,
    )
    pair_w.start()
    pair_b.start()

    with scope("own3"):
        hown[...] = tn(adj[:nodes, :], ybuf[...])

    with scope("pairwait"):
        pair_w.wait()
        pair_b.wait()
    rs_send[...] = (wpart[mine, :] + wpair[...].astype(F32)).astype(rs_send.dtype).reshape(rs_send.shape)
    bsum[...] = bpart[...] + bpair[...]

    def scatter(a, b):
        pltpu.make_async_remote_copy(
            src_ref=rs_send.at[lax.div(a * n_sub + b, 2)],
            dst_ref=rs_recv.at[chip],
            send_sem=ssem.at[8],
            recv_sem=rsem.at[8],
            device_id=(a, b),
            device_id_type=MESH,
        ).start()

    with scope("scatter"):
        each(scatter, False)
        own_rs = pltpu.make_async_copy(rs_send.at[chip], rs_recv.at[chip], loc_sem.at[6])
        own_rs.start()

    hm = arrive(4)
    fill(5, hown[nodes:, :] + tn(adj[nodes:, nodes:], hm))
    exchange(5)
    with scope("own4"):
        hown[:nodes, :] += tn(adj[nodes:, :nodes], hm)
        zbuf[...] = nt(gzbuf[...], wts[0])

    def spread_bias(a, b):
        pltpu.make_async_remote_copy(
            src_ref=bsum,
            dst_ref=brecv.at[chip],
            send_sem=ssem.at[9],
            recv_sem=rsem.at[9],
            device_id=(a, b),
            device_id_type=MESH,
        ).start()

    with scope("bias"):
        each(spread_bias, False)
        own_b = pltpu.make_async_copy(bsum, brecv.at[chip], loc_sem.at[7])
        own_b.start()

    with scope("rswait"):
        own_rs.wait()
        others = rs_recv.at[pl.ds(0, n_chip - 1)]
        pltpu.make_async_copy(others, others, rsem.at[8]).wait()
    ag_send[...] = (jnp.sum(rs_recv[...].astype(F32), axis=0) * norm_factor).astype(ag_send.dtype)

    def gather(a, b):
        pltpu.make_async_remote_copy(
            src_ref=ag_send,
            dst_ref=ag_all.at[core, chip],
            send_sem=ssem.at[10],
            recv_sem=rsem.at[10],
            device_id=(a, b),
            device_id_type=MESH,
        ).start()

    with scope("gather"):
        each(gather, False)
        own_ag = pltpu.make_async_copy(ag_send, ag_all.at[core, chip], loc_sem.at[8])
        own_ag.start()

    hm2 = arrive(5)
    with scope("last"):

        for i in range(nodes // big):
            here = pl.ds(i * big, big)
            hsum = (hown[here, :] + nn(place[here, :], hm2)).astype(BF16)
            gfeat_ref[here, :] = (zbuf[here, :] + nt(hsum, wts[1])).astype(BF16)

    with scope("agwait"):
        own_ag.wait()
        others = ag_all.at[core, pl.ds(0, n_chip - 1)]
        pltpu.make_async_copy(others, others, rsem.at[10]).wait()
    own_b.wait()
    others = brecv.at[pl.ds(0, n_chip - 1)]
    pltpu.make_async_copy(others, others, rsem.at[9]).wait()
    gb_ref[...] = jnp.sum(brecv[...], axis=0) * norm_factor
    swap = pltpu.make_async_remote_copy(
        src_ref=ag_all.at[core],
        dst_ref=ag_all.at[core],
        send_sem=ssem.at[11],
        recv_sem=rsem.at[11],
        device_id=partner,
        device_id_type=MESH,
    )
    with scope("swap"):
        swap.start()
        swap.wait()
    gw_ref[...] = ag_all[...].astype(F32).reshape(4 * dim, dim)

    with scope("drain"):
        for k in range(6):
            sent(k)
        for ref, k in ((rs_send, 8), (brecv, 9)):
            others = ref.at[pl.ds(0, n_chip - 1)]
            pltpu.make_async_copy(others, others, ssem.at[k]).wait()
        others = ag_all.at[core, pl.ds(0, n_chip - 1)]
        pltpu.make_async_copy(others, others, ssem.at[10]).wait()


def put(*refs):
    sem = refs[-1]
    half = len(refs) // 2
    copies = [
        pltpu.make_async_copy(a, b, sem.at[i])
        for i, (a, b) in enumerate(zip(refs[:half], refs[half:-1]))
    ]
    for c in copies:
        c.start()
    for c in copies:
        c.wait()


def shards(
    n_dom,
    n_sub,
    features,
    cotangent,
    w_self_one,
    w_nbr_one,
    bias_one,
    w_self_two,
    w_nbr_two,
    in_count,
    send_list,
    src_slot,
    dst_slot,
    edge_count,
):
    nodes, dim = features.shape
    n_dev = n_dom * n_sub
    n_chip = n_dev // 2
    per_peer = send_list.shape[2]
    n_mir = n_dev * per_peer
    slots = nodes + n_mir
    edges = src_slot.shape[1]
    own_rows = 2 * dim // n_chip
    vm = pl.BlockSpec(memory_space=pltpu.VMEM)
    hbm = pl.BlockSpec(memory_space=pltpu.HBM)
    norm_factor = float(nodes * n_dev) ** -0.5
    full = pltpu.VMEM((nodes, dim), F32)
    fullb = pltpu.VMEM((nodes, dim), BF16)
    allf = pltpu.VMEM((slots, dim), F32)
    msgs = pltpu.VMEM((6, n_dev, per_peer, dim), BF16)
    rs_t = BF16
    ag_t = BF16
    gfeat, gw, gb = pl.pallas_call(
        functools.partial(kernel, n_dom, n_sub, norm_factor),
        out_shape=(
            jax.ShapeDtypeStruct((nodes, dim), BF16),
            jax.ShapeDtypeStruct((4 * dim, dim), F32),
            jax.ShapeDtypeStruct((1, dim), F32),
        ),
        in_specs=[hbm] * 12,
        out_specs=(vm, vm, vm),
        scratch_shapes=[
            pltpu.VMEM((1, 1), jnp.int32),
            pltpu.VMEM((1, edges), jnp.int32),
            pltpu.VMEM((1, edges), jnp.int32),
            pltpu.VMEM((per_peer, n_dev), jnp.int32),
            pltpu.VMEM((1, nodes), jnp.int32),
            pltpu.VMEM((1, dim), F32),
            fullb,
            fullb,
            pltpu.VMEM((4, dim, dim), BF16),
            pltpu.VMEM((slots, edges), ONE_HOT),
            pltpu.VMEM((slots, edges), ONE_HOT),
            pltpu.VMEM((slots, slots), BF16),
            pltpu.VMEM((nodes, n_mir), BF16),
            pltpu.VMEM((n_mir, nodes), BF16),
            full,
            fullb,
            full,
            full,
            allf,
            allf,
            allf,
            fullb,
            fullb,
            fullb,
            fullb,
            msgs,
            msgs,
            pltpu.VMEM((4 * dim, dim), F32),
            pltpu.VMEM((1, dim), F32),
            pltpu.VMEM((2 * dim, dim), BF16),
            pltpu.VMEM((2 * dim, dim), BF16),
            pltpu.VMEM((1, dim), F32),
            pltpu.VMEM((1, dim), F32),
            pltpu.VMEM((n_chip, 1, dim), F32),
            pltpu.VMEM((n_chip, own_rows, dim), rs_t),
            pltpu.VMEM((n_chip, own_rows, dim), rs_t),
            pltpu.VMEM((own_rows, dim), ag_t),
            pltpu.VMEM((2, n_chip, own_rows, dim), ag_t),
            pltpu.SemaphoreType.DMA((12,)),
            pltpu.SemaphoreType.DMA((9,)),
            pltpu.SemaphoreType.DMA((12,)),
            pltpu.SemaphoreType.DMA((12,)),
        ],
        compiler_params=pltpu.CompilerParams(
            collective_id=0, has_side_effects=True, vmem_limit_bytes=44 << 20
        ),
    )(
        edge_count.reshape(1, 1),
        *(
            pltpu.with_memory_space_constraint(x, pltpu.HBM)
            for x in (
                src_slot,
                dst_slot,
                send_list[0].T,
                in_count.reshape(1, nodes),
                bias_one.reshape(1, dim),
                features,
                cotangent,
                w_self_one,
                w_nbr_one,
                w_self_two,
                w_nbr_two,
            )
        ),
    )
    results = (gfeat, gw, gb)
    gfeat, gw, gb = pl.pallas_call(
        put,
        out_shape=tuple(jax.ShapeDtypeStruct(x.shape, x.dtype) for x in results),
        in_specs=[vm] * 3,
        out_specs=(hbm,) * 3,
        scratch_shapes=[pltpu.SemaphoreType.DMA((3,))],
        compiler_params=pltpu.CompilerParams(vmem_limit_bytes=1 << 20),
    )(*results)
    return gfeat, gw.reshape(4, dim, dim), gb.reshape(dim)


def solution(mesh):
    both = ("dom", "sub")
    return jax.shard_map(
        functools.partial(shards, mesh.shape["dom"], mesh.shape["sub"]),
        mesh=mesh,
        in_specs=(
            P(both, None),
            P(both, None),
            P(),
            P(),
            P(),
            P(),
            P(),
            P(both),
            P(both, None, None),
            P(both, None),
            P(both, None),
            P(both),
        ),
        out_specs=(P(both, None), P(), P()),
        check_vma=False,
    )
```

```python
import contextlib
import functools

import jax
import jax.numpy as jnp
from jax import lax
from jax.experimental import pallas as pl
from jax.experimental.pallas import tpu as pltpu
from jax.sharding import PartitionSpec as P

MESH = pl.DeviceIdType.MESH
F32 = jnp.float32
BF16 = jnp.bfloat16
ONE_HOT = jnp.float8_e4m3fn
FAR = (10, 9, 11, 6, 14, 8, 2, 5, 7, 13, 15, 4, 12, 1, 3)


def scope(name):
    return contextlib.nullcontext()


def nn(left, right):
    return jnp.dot(left, right, preferred_element_type=F32)


def tn(left, right):
    return lax.dot_general(left, right, (((0,), (0,)), ((), ())), preferred_element_type=F32)


def nt(left, right):
    return lax.dot_general(left, right, (((1,), (1,)), ((), ())), preferred_element_type=F32)


def digits(codes):
    total = 0
    for code in reversed(codes):
        total = total * 16 + code
    return total


def wrap4(v):
    return jnp.where(v >= 4, v - 4, v)


def kernel(
    n_dom,
    n_sub,
    norm_factor,
    count_hbm,
    src_hbm,
    dst_hbm,
    send_hbm,
    in_count_hbm,
    bias_hbm,
    feat_hbm,
    cot_hbm,
    ws1_hbm,
    wn1_hbm,
    ws2_hbm,
    wn2_hbm,
    gfeat_ref,
    gw_ref,
    gb_ref,
    count_ref,
    src_ref,
    dst_ref,
    send_ref,
    in_count_ref,
    bias_ref,
    feat,
    cot,
    wts,
    src_hot,
    dst_hot,
    adj,
    place,
    picks,
    inv,
    ybuf,
    zbuf,
    gbuf,
    fown,
    gown,
    hown,
    mbuf,
    hbuf,
    gzbuf,
    gsbuf,
    sends,
    recvs,
    wpart,
    bpart,
    wsend,
    wpair,
    bpair,
    bsum,
    brecv,
    rs_send,
    rs_recv,
    ag_send,
    ag_all,
    in_sem,
    loc_sem,
    ssem,
    rsem,
    bsem,
):
    nodes, dim = feat.shape
    n_dev = n_dom * n_sub
    n_chip = n_dev // 2
    n_mir = place.shape[1]
    slots = nodes + n_mir
    per_peer = n_mir // n_dev
    half = wpair.shape[0]
    blk = 256
    d = lax.axis_index("dom")
    s = lax.axis_index("sub")
    me = d * n_sub + s
    chip = lax.div(me, 2)
    core = lax.rem(me, 2)
    at_y, at_z, at_x = lax.div(d, 4), lax.rem(d, 4), lax.div(s, 2)
    partner = (d, s + 1 - 2 * core)

    small = [
        (send_hbm, send_ref),
        (in_count_hbm, in_count_ref),
        (count_hbm, count_ref),
        (src_hbm, src_ref),
        (dst_hbm, dst_ref),
        (bias_hbm, bias_ref),
    ]
    large = [
        (feat_hbm, feat),
        (cot_hbm, cot),
        (ws1_hbm, wts.at[0]),
        (wn1_hbm, wts.at[1]),
        (ws2_hbm, wts.at[2]),
        (wn2_hbm, wts.at[3]),
    ]
    loads = [
        pltpu.make_async_copy(a, b, in_sem.at[i]) for i, (a, b) in enumerate(small + large)
    ]
    for c in loads:
        c.start()

    xs = [wrap4(at_x + k) * 2 for k in (2, 1, 3, 0)]
    cores = [1 - core, core]

    def each(do, both):
        def line(dom, is_mine):
            for k in range(4):
                for j in range(2):
                    if (both or j == 1) and not (is_mine and k == 3 and j == 1):
                        do(dom, xs[k] + cores[j])

        def dom_of(code):
            return wrap4(at_y + lax.div(code, 4)) * 4 + wrap4(at_z + lax.rem(code, 4))

        def turn(_, left):
            line(dom_of(lax.rem(left, 16)), False)
            return lax.div(left, 16)

        lax.fori_loop(0, 7, turn, jnp.int32(digits(FAR[:7])))
        lax.fori_loop(0, 7, turn, jnp.int32(digits(FAR[7:14])))
        line(dom_of(jnp.int32(FAR[14])), False)
        line(d, True)

    barrier = pltpu.get_barrier_semaphore()
    with scope("greet"):
        each(
            lambda a, b: pl.semaphore_signal(barrier, 1, device_id=(a, b), device_id_type=MESH),
            True,
        )

    def exchange(k):
        def one(a, b):
            pltpu.make_async_remote_copy(
                src_ref=sends.at[k, a * n_sub + b],
                dst_ref=recvs.at[k, me],
                send_sem=ssem.at[k],
                recv_sem=rsem.at[k],
                device_id=(a, b),
                device_id_type=MESH,
            ).start()

        with scope(f"ex{k}"):
            each(one, True)
            pltpu.make_async_copy(sends.at[k, me], recvs.at[k, me], loc_sem.at[k]).start()

    def arrive(k):
        with scope(f"arr{k}"):
            pltpu.make_async_copy(sends.at[k, me], recvs.at[k, me], loc_sem.at[k]).wait()
            all_in = recvs.at[k, pl.ds(0, n_dev - 1)]
            pltpu.make_async_copy(all_in, all_in, rsem.at[k]).wait()
        return recvs[k].reshape(n_mir, dim)

    def sent(k):
        all_out = sends.at[k, pl.ds(0, n_dev - 1)]
        pltpu.make_async_copy(all_out, all_out, ssem.at[k]).wait()

    def rows(ref, i):
        return ref.at[pl.ds(pl.multiple_of(i * blk, blk), blk), :]

    def fill(k, value):
        sends[k] = value.astype(BF16).reshape(n_dev, per_peer, dim)

    def hot_block(index_row, i):
        shape = (blk, index_row.shape[1])
        ids = lax.broadcasted_iota(jnp.int32, shape, 0).astype(F32).astype(BF16)
        here = (index_row - i * blk).astype(F32).astype(BF16)
        return jnp.where(ids == here, jnp.ones(shape, BF16), jnp.zeros(shape, BF16))

    with scope("prepf"):
        loads[0].wait()
        lists = send_ref[...]
        parts = jnp.concatenate([lists // 32, lists % 32], axis=0).astype(F32).astype(BF16)
        lane = lax.broadcasted_iota(jnp.int32, (n_dev, n_mir), 1)
        widen = (
            lax.shift_right_logical(lane, 2) == lax.broadcasted_iota(jnp.int32, (n_dev, n_mir), 0)
        ).astype(BF16)
        wide = nn(parts, widen)
        wide = wide[:per_peer] * 32.0 + wide[per_peer:]
        turn_of = lax.broadcasted_iota(jnp.int32, (per_peer, n_mir), 1) & 3
        mine_of = turn_of == lax.broadcasted_iota(jnp.int32, (per_peer, n_mir), 0)
        picked = jnp.sum(jnp.where(mine_of, wide, 0.0), axis=0, keepdims=True).astype(jnp.int32)
        for i in range(nodes // blk):
            place[pl.ds(i * blk, blk), :] = hot_block(picked, i)
        picks[...] = place[...].T
        loads[6].wait()
        fill(0, nn(picks[...], feat[...]))

    with scope("hot"):
        for c in loads[2:6]:
            c.wait()
        edges = src_ref.shape[1]
        live = lax.broadcasted_iota(jnp.int32, (1, edges), 1) < count_ref[...]
        src_row = jnp.where(live, src_ref[...], -1)
        dst_row = jnp.where(live, dst_ref[...], -1)

        def hot(i, _):
            rows(src_hot, i)[...] = hot_block(src_row, i).astype(ONE_HOT)
            rows(dst_hot, i)[...] = hot_block(dst_row, i).astype(ONE_HOT)
            return 0

        lax.fori_loop(0, slots // blk, hot, 0)

    with scope("bwait"):
        pl.semaphore_wait(barrier, n_dev - 1)
    exchange(0)

    with scope("prepg"):
        loads[1].wait()
        inv_row = 1.0 / jnp.maximum(in_count_ref[...], 1).astype(F32)
        inv_col = jnp.broadcast_to(inv_row, (128, nodes)).T
        inv[...] = jnp.concatenate([inv_col] * (dim // 128), axis=1)
        loads[7].wait()
        ybuf[...] = (cot[...].astype(F32) * inv[...]).astype(BF16)
        fill(1, nn(picks[...], ybuf[...]))
    exchange(1)

    masters = nodes // blk
    with scope("buildm"):

        def build_rows(i, _):
            rows(adj, i)[...] = nt(rows(dst_hot, i)[...], src_hot[...]).astype(BF16)
            return 0

        lax.fori_loop(masters, slots // blk, build_rows, 0)

        def build_columns(i, _):
            here = pl.ds(pl.multiple_of(i * blk, blk), blk)
            adj[here, nodes:] = nt(dst_hot[here, :], src_hot[nodes:, :]).astype(BF16)
            return 0

        lax.fori_loop(0, masters, build_columns, 0)

    with scope("own1"):
        fown[nodes:, :] = nn(adj[nodes:, :nodes], feat[...])
        gown[nodes:, :] = tn(adj[:nodes, nodes:], ybuf[...])
        for c in loads[8:]:
            c.wait()
        zbuf[...] = nn(feat[...], wts[0]) + bias_ref[...]
        gbuf[...] = nt(cot[...], wts[2])

    fm = arrive(0)
    fill(2, fown[nodes:, :] + nn(adj[nodes:, nodes:], fm))
    exchange(2)
    gm = arrive(1)
    fill(3, gown[nodes:, :] + tn(adj[nodes:, nodes:], gm))
    exchange(3)

    with scope("buildo"):

        def build_rest(i, _):
            here = pl.ds(pl.multiple_of(i * blk, blk), blk)
            adj[here, :nodes] = nt(dst_hot[here, :], src_hot[:nodes, :]).astype(BF16)
            return 0

        lax.fori_loop(0, masters, build_rest, 0)
    with scope("own2"):
        fown[:nodes, :] = nn(adj[:nodes, :nodes], feat[...]) + nn(adj[:nodes, nodes:], fm)
        gown[:nodes, :] = tn(adj[:nodes, :nodes], ybuf[...]) + tn(adj[nodes:, :nodes], gm)

    big = nodes // 2
    fm2 = arrive(2)
    with scope("dense1"):
        for i in range(nodes // big):
            here = pl.ds(i * big, big)
            mean = ((fown[here, :] + nn(place[here, :], fm2)) * inv[here, :]).astype(BF16)
            mbuf[here, :] = mean
            z = zbuf[here, :] + nn(mean, wts[1])
            sig = 1.0 / (1.0 + jnp.exp(-z))
            hbuf[here, :] = (z * sig).astype(BF16)
            zbuf[here, :] = sig * (1.0 + z * (1.0 - sig))
        wpart[pl.ds(2 * dim, dim), :] = tn(hbuf[...], cot[...])

    gm2 = arrive(3)
    with scope("dense2"):
        bias_sum = jnp.zeros((1, dim), F32)
        for i in range(nodes // big):
            here = pl.ds(i * big, big)
            gsum = (gown[here, :] + nn(place[here, :], gm2)).astype(BF16)
            gsbuf[here, :] = gsum
            gh = gbuf[here, :] + nt(gsum, wts[3])
            gz = (gh * zbuf[here, :]).astype(BF16)
            gzbuf[here, :] = gz
            gzf = gz.astype(F32)
            ybuf[here, :] = (gzf * inv[here, :]).astype(BF16)
            bias_sum += jnp.sum(gzf, axis=0, keepdims=True)
        bpart[...] = bias_sum

    with scope("pick3"):
        fill(4, nn(picks[...], ybuf[...]))
    exchange(4)

    with scope("wgrad"):
        wpart[pl.ds(0, dim), :] = tn(feat[...], gzbuf[...])
        wpart[pl.ds(dim, dim), :] = tn(mbuf[...], gzbuf[...])
        wpart[pl.ds(3 * dim, dim), :] = tn(hbuf[...], gsbuf[...])
    mine = pl.ds(pl.multiple_of(core * half, half), half)
    other = pl.ds(pl.multiple_of((1 - core) * half, half), half)
    wsend[...] = wpart[other, :].astype(BF16)
    pair_w = pltpu.make_async_remote_copy(
        src_ref=wsend,
        dst_ref=wpair,
        send_sem=ssem.at[6],
        recv_sem=rsem.at[6],
        device_id=partner,
        device_id_type=MESH,
    )
    pair_b = pltpu.make_async_remote_copy(
        src_ref=bpart,
        dst_ref=bpair,
        send_sem=ssem.at[7],
        recv_sem=rsem.at[7],
        device_id=partner,
        device_id_type=MESH,
    )
    pair_w.start()
    pair_b.start()

    with scope("own3"):
        hown[...] = tn(adj[:nodes, :], ybuf[...])

    with scope("pairwait"):
        pair_w.wait()
        pair_b.wait()
    rs_send[...] = (wpart[mine, :] + wpair[...].astype(F32)).astype(rs_send.dtype).reshape(rs_send.shape)
    bias_pair = bpart[...] + bpair[...]

    places = (at_x, at_z, at_y)

    def bias_out(stage, value):
        bsum[stage] = value
        brecv[stage, places[stage]] = value
        for k in (2, 1, 3):
            to = (
                (d, wrap4(at_x + k) * 2 + core),
                (at_y * 4 + wrap4(at_z + k), s),
                (wrap4(at_y + k) * 4 + at_z, s),
            )[stage]
            pltpu.make_async_remote_copy(
                src_ref=bsum.at[stage],
                dst_ref=brecv.at[stage, places[stage]],
                send_sem=bsem.at[0, stage],
                recv_sem=bsem.at[1, stage],
                device_id=to,
                device_id_type=MESH,
            ).start()

    def bias_in(stage):
        others = brecv.at[stage, pl.ds(0, 3)]
        pltpu.make_async_copy(others, others, bsem.at[1, stage]).wait()
        return jnp.sum(brecv[stage], axis=0)

    def scatter(a, b):
        pltpu.make_async_remote_copy(
            src_ref=rs_send.at[lax.div(a * n_sub + b, 2)],
            dst_ref=rs_recv.at[chip],
            send_sem=ssem.at[8],
            recv_sem=rsem.at[8],
            device_id=(a, b),
            device_id_type=MESH,
        ).start()

    bias_out(0, bias_pair)
    with scope("scatter"):
        each(scatter, False)
        own_rs = pltpu.make_async_copy(rs_send.at[chip], rs_recv.at[chip], loc_sem.at[6])
        own_rs.start()

    hm = arrive(4)
    bias_out(1, bias_in(0))
    fill(5, hown[nodes:, :] + tn(adj[nodes:, nodes:], hm))
    exchange(5)
    with scope("own4"):
        hown[:nodes, :] += tn(adj[nodes:, :nodes], hm)
        zbuf[...] = nt(gzbuf[...], wts[0])

    with scope("rswait"):
        own_rs.wait()
        others = rs_recv.at[pl.ds(0, n_chip - 1)]
        pltpu.make_async_copy(others, others, rsem.at[8]).wait()
    ag_send[...] = (jnp.sum(rs_recv[...].astype(F32), axis=0) * norm_factor).astype(ag_send.dtype)

    def gather(a, b):
        pltpu.make_async_remote_copy(
            src_ref=ag_send,
            dst_ref=ag_all.at[core, chip],
            send_sem=ssem.at[10],
            recv_sem=rsem.at[10],
            device_id=(a, b),
            device_id_type=MESH,
        ).start()

    bias_out(2, bias_in(1))
    with scope("gather"):
        each(gather, False)
        own_ag = pltpu.make_async_copy(ag_send, ag_all.at[core, chip], loc_sem.at[8])
        own_ag.start()

    hm2 = arrive(5)
    with scope("last"):

        for i in range(nodes // big):
            here = pl.ds(i * big, big)
            hsum = (hown[here, :] + nn(place[here, :], hm2)).astype(BF16)
            gfeat_ref[here, :] = (zbuf[here, :] + nt(hsum, wts[1])).astype(BF16)

    with scope("agwait"):
        own_ag.wait()
        others = ag_all.at[core, pl.ds(0, n_chip - 1)]
        pltpu.make_async_copy(others, others, rsem.at[10]).wait()
    swap = pltpu.make_async_remote_copy(
        src_ref=ag_all.at[core],
        dst_ref=ag_all.at[core],
        send_sem=ssem.at[11],
        recv_sem=rsem.at[11],
        device_id=partner,
        device_id_type=MESH,
    )
    with scope("swap"):
        swap.start()
        gb_ref[...] = bias_in(2) * norm_factor
        swap.wait()
    gw_ref[...] = ag_all[...].astype(F32).reshape(4 * dim, dim)

    with scope("drain"):
        for k in range(6):
            sent(k)
        others = rs_send.at[pl.ds(0, n_chip - 1)]
        pltpu.make_async_copy(others, others, ssem.at[8]).wait()
        for stage in range(3):
            others = brecv.at[stage, pl.ds(0, 3)]
            pltpu.make_async_copy(others, others, bsem.at[0, stage]).wait()
        others = ag_all.at[core, pl.ds(0, n_chip - 1)]
        pltpu.make_async_copy(others, others, ssem.at[10]).wait()


def put(*refs):
    sem = refs[-1]
    half = len(refs) // 2
    copies = [
        pltpu.make_async_copy(a, b, sem.at[i])
        for i, (a, b) in enumerate(zip(refs[:half], refs[half:-1]))
    ]
    for c in copies:
        c.start()
    for c in copies:
        c.wait()


def shards(
    n_dom,
    n_sub,
    features,
    cotangent,
    w_self_one,
    w_nbr_one,
    bias_one,
    w_self_two,
    w_nbr_two,
    in_count,
    send_list,
    src_slot,
    dst_slot,
    edge_count,
):
    nodes, dim = features.shape
    n_dev = n_dom * n_sub
    n_chip = n_dev // 2
    per_peer = send_list.shape[2]
    n_mir = n_dev * per_peer
    slots = nodes + n_mir
    edges = src_slot.shape[1]
    own_rows = 2 * dim // n_chip
    vm = pl.BlockSpec(memory_space=pltpu.VMEM)
    hbm = pl.BlockSpec(memory_space=pltpu.HBM)
    norm_factor = float(nodes * n_dev) ** -0.5
    full = pltpu.VMEM((nodes, dim), F32)
    fullb = pltpu.VMEM((nodes, dim), BF16)
    allf = pltpu.VMEM((slots, dim), F32)
    msgs = pltpu.VMEM((6, n_dev, per_peer, dim), BF16)
    rs_t = BF16
    ag_t = BF16
    gfeat, gw, gb = pl.pallas_call(
        functools.partial(kernel, n_dom, n_sub, norm_factor),
        out_shape=(
            jax.ShapeDtypeStruct((nodes, dim), BF16),
            jax.ShapeDtypeStruct((4 * dim, dim), F32),
            jax.ShapeDtypeStruct((1, dim), F32),
        ),
        in_specs=[hbm] * 12,
        out_specs=(vm, vm, vm),
        scratch_shapes=[
            pltpu.VMEM((1, 1), jnp.int32),
            pltpu.VMEM((1, edges), jnp.int32),
            pltpu.VMEM((1, edges), jnp.int32),
            pltpu.VMEM((per_peer, n_dev), jnp.int32),
            pltpu.VMEM((1, nodes), jnp.int32),
            pltpu.VMEM((1, dim), F32),
            fullb,
            fullb,
            pltpu.VMEM((4, dim, dim), BF16),
            pltpu.VMEM((slots, edges), ONE_HOT),
            pltpu.VMEM((slots, edges), ONE_HOT),
            pltpu.VMEM((slots, slots), BF16),
            pltpu.VMEM((nodes, n_mir), BF16),
            pltpu.VMEM((n_mir, nodes), BF16),
            full,
            fullb,
            full,
            full,
            allf,
            allf,
            allf,
            fullb,
            fullb,
            fullb,
            fullb,
            msgs,
            msgs,
            pltpu.VMEM((4 * dim, dim), F32),
            pltpu.VMEM((1, dim), F32),
            pltpu.VMEM((2 * dim, dim), BF16),
            pltpu.VMEM((2 * dim, dim), BF16),
            pltpu.VMEM((1, dim), F32),
            pltpu.VMEM((3, 1, dim), F32),
            pltpu.VMEM((3, 4, 1, dim), F32),
            pltpu.VMEM((n_chip, own_rows, dim), rs_t),
            pltpu.VMEM((n_chip, own_rows, dim), rs_t),
            pltpu.VMEM((own_rows, dim), ag_t),
            pltpu.VMEM((2, n_chip, own_rows, dim), ag_t),
            pltpu.SemaphoreType.DMA((12,)),
            pltpu.SemaphoreType.DMA((9,)),
            pltpu.SemaphoreType.DMA((12,)),
            pltpu.SemaphoreType.DMA((12,)),
            pltpu.SemaphoreType.DMA((2, 3)),
        ],
        compiler_params=pltpu.CompilerParams(
            collective_id=0, has_side_effects=True, vmem_limit_bytes=44 << 20
        ),
    )(
        edge_count.reshape(1, 1),
        *(
            pltpu.with_memory_space_constraint(x, pltpu.HBM)
            for x in (
                src_slot,
                dst_slot,
                send_list[0].T,
                in_count.reshape(1, nodes),
                bias_one.reshape(1, dim),
                features,
                cotangent,
                w_self_one,
                w_nbr_one,
                w_self_two,
                w_nbr_two,
            )
        ),
    )
    results = (gfeat, gw, gb)
    gfeat, gw, gb = pl.pallas_call(
        put,
        out_shape=tuple(jax.ShapeDtypeStruct(x.shape, x.dtype) for x in results),
        in_specs=[vm] * 3,
        out_specs=(hbm,) * 3,
        scratch_shapes=[pltpu.SemaphoreType.DMA((3,))],
        compiler_params=pltpu.CompilerParams(vmem_limit_bytes=1 << 20),
    )(*results)
    return gfeat, gw.reshape(4, dim, dim), gb.reshape(dim)


def solution(mesh):
    both = ("dom", "sub")
    return jax.shard_map(
        functools.partial(shards, mesh.shape["dom"], mesh.shape["sub"]),
        mesh=mesh,
        in_specs=(
            P(both, None),
            P(both, None),
            P(),
            P(),
            P(),
            P(),
            P(),
            P(both),
            P(both, None, None),
            P(both, None),
            P(both, None),
            P(both),
        ),
        out_specs=(P(both, None), P(), P()),
        check_vma=False,
    )
```

```python
import contextlib
import functools

import jax
import jax.numpy as jnp
from jax import lax
from jax.experimental import pallas as pl
from jax.experimental.pallas import tpu as pltpu
from jax.sharding import PartitionSpec as P

MESH = pl.DeviceIdType.MESH
F32 = jnp.float32
BF16 = jnp.bfloat16
ONE_HOT = jnp.float8_e4m3fn
FAR = (10, 9, 11, 6, 14, 8, 2, 5, 7, 13, 15, 4, 12, 1, 3)


def scope(name):
    return contextlib.nullcontext()


def nn(left, right):
    return jnp.dot(left, right, preferred_element_type=F32)


def tn(left, right):
    return lax.dot_general(left, right, (((0,), (0,)), ((), ())), preferred_element_type=F32)


def nt(left, right):
    return lax.dot_general(left, right, (((1,), (1,)), ((), ())), preferred_element_type=F32)


def digits(codes):
    total = 0
    for code in reversed(codes):
        total = total * 16 + code
    return total


def wrap4(v):
    return jnp.where(v >= 4, v - 4, v)


def kernel(
    n_dom,
    n_sub,
    norm_factor,
    count_hbm,
    src_hbm,
    dst_hbm,
    send_hbm,
    in_count_hbm,
    bias_hbm,
    feat_hbm,
    cot_hbm,
    ws1_hbm,
    wn1_hbm,
    ws2_hbm,
    wn2_hbm,
    gfeat_ref,
    gw_ref,
    gb_ref,
    count_ref,
    src_ref,
    dst_ref,
    send_ref,
    in_count_ref,
    bias_ref,
    feat,
    cot,
    wts,
    src_hot,
    dst_hot,
    adj,
    place,
    picks,
    inv,
    ybuf,
    zbuf,
    gbuf,
    fown,
    gown,
    hown,
    mbuf,
    hbuf,
    gzbuf,
    gsbuf,
    sends,
    recvs,
    wpart,
    bpart,
    wsend,
    wpair,
    bpair,
    bsum,
    brecv,
    rs_send,
    rs_recv,
    ag_send,
    ag_all,
    in_sem,
    loc_sem,
    ssem,
    rsem,
    bsem,
):
    nodes, dim = feat.shape
    n_dev = n_dom * n_sub
    n_chip = n_dev // 2
    n_mir = place.shape[1]
    slots = nodes + n_mir
    per_peer = n_mir // n_dev
    half = wpair.shape[0]
    blk = 256
    d = lax.axis_index("dom")
    s = lax.axis_index("sub")
    me = d * n_sub + s
    chip = lax.div(me, 2)
    core = lax.rem(me, 2)
    at_y, at_z, at_x = lax.div(d, 4), lax.rem(d, 4), lax.div(s, 2)
    partner = (d, s + 1 - 2 * core)

    small = [
        (send_hbm, send_ref),
        (in_count_hbm, in_count_ref),
        (count_hbm, count_ref),
        (src_hbm, src_ref),
        (dst_hbm, dst_ref),
        (bias_hbm, bias_ref),
    ]
    large = [
        (feat_hbm, feat),
        (cot_hbm, cot),
        (ws1_hbm, wts.at[0]),
        (wn1_hbm, wts.at[1]),
        (ws2_hbm, wts.at[2]),
        (wn2_hbm, wts.at[3]),
    ]
    loads = [
        pltpu.make_async_copy(a, b, in_sem.at[i]) for i, (a, b) in enumerate(small + large)
    ]
    for c in loads:
        c.start()

    xs = [wrap4(at_x + k) * 2 for k in (2, 1, 3, 0)]
    cores = [1 - core, core]

    def each(do, both):
        def line(dom, is_mine):
            for k in range(4):
                for j in range(2):
                    if (both or j == 1) and not (is_mine and k == 3 and j == 1):
                        do(dom, xs[k] + cores[j])

        def dom_of(code):
            return wrap4(at_y + lax.div(code, 4)) * 4 + wrap4(at_z + lax.rem(code, 4))

        def turn(_, left):
            line(dom_of(lax.rem(left, 16)), False)
            return lax.div(left, 16)

        lax.fori_loop(0, 7, turn, jnp.int32(digits(FAR[:7])))
        lax.fori_loop(0, 7, turn, jnp.int32(digits(FAR[7:14])))
        line(dom_of(jnp.int32(FAR[14])), False)
        line(d, True)

    barrier = pltpu.get_barrier_semaphore()
    with scope("greet"):
        each(
            lambda a, b: pl.semaphore_signal(barrier, 1, device_id=(a, b), device_id_type=MESH),
            True,
        )

    def exchange(k):
        def one(a, b):
            pltpu.make_async_remote_copy(
                src_ref=sends.at[k, a * n_sub + b],
                dst_ref=recvs.at[k, me],
                send_sem=ssem.at[k],
                recv_sem=rsem.at[k],
                device_id=(a, b),
                device_id_type=MESH,
            ).start()

        with scope(f"ex{k}"):
            each(one, True)
            pltpu.make_async_copy(sends.at[k, me], recvs.at[k, me], loc_sem.at[k]).start()

    def arrive(k):
        with scope(f"arr{k}"):
            pltpu.make_async_copy(sends.at[k, me], recvs.at[k, me], loc_sem.at[k]).wait()
            all_in = recvs.at[k, pl.ds(0, n_dev - 1)]
            pltpu.make_async_copy(all_in, all_in, rsem.at[k]).wait()
        return recvs[k].reshape(n_mir, dim)

    def sent(k):
        all_out = sends.at[k, pl.ds(0, n_dev - 1)]
        pltpu.make_async_copy(all_out, all_out, ssem.at[k]).wait()

    def rows(ref, i):
        return ref.at[pl.ds(pl.multiple_of(i * blk, blk), blk), :]

    def fill(k, value):
        sends[k] = value.astype(BF16).reshape(n_dev, per_peer, dim)

    def hot_block(index_row, i):
        shape = (blk, index_row.shape[1])
        ids = lax.broadcasted_iota(jnp.int32, shape, 0).astype(F32).astype(BF16)
        here = (index_row - i * blk).astype(F32).astype(BF16)
        return jnp.where(ids == here, jnp.ones(shape, BF16), jnp.zeros(shape, BF16))

    with scope("prepf"):
        loads[0].wait()
        lists = send_ref[...]
        parts = jnp.concatenate([lists // 32, lists % 32], axis=0).astype(F32).astype(BF16)
        lane = lax.broadcasted_iota(jnp.int32, (n_dev, n_mir), 1)
        widen = (
            lax.shift_right_logical(lane, 2) == lax.broadcasted_iota(jnp.int32, (n_dev, n_mir), 0)
        ).astype(BF16)
        wide = nn(parts, widen)
        wide = wide[:per_peer] * 32.0 + wide[per_peer:]
        turn_of = lax.broadcasted_iota(jnp.int32, (per_peer, n_mir), 1) & 3
        mine_of = turn_of == lax.broadcasted_iota(jnp.int32, (per_peer, n_mir), 0)
        picked = jnp.sum(jnp.where(mine_of, wide, 0.0), axis=0, keepdims=True).astype(jnp.int32)
        for i in range(nodes // blk):
            place[pl.ds(i * blk, blk), :] = hot_block(picked, i)
        picks[...] = place[...].T
        loads[6].wait()
        fill(0, nn(picks[...], feat[...]))

    with scope("hot"):
        for c in loads[2:6]:
            c.wait()
        edges = src_ref.shape[1]
        live = lax.broadcasted_iota(jnp.int32, (1, edges), 1) < count_ref[...]
        src_row = jnp.where(live, src_ref[...], -1)
        dst_row = jnp.where(live, dst_ref[...], -1)

        def hot(i, _):
            rows(src_hot, i)[...] = hot_block(src_row, i).astype(ONE_HOT)
            rows(dst_hot, i)[...] = hot_block(dst_row, i).astype(ONE_HOT)
            return 0

        lax.fori_loop(0, slots // blk, hot, 0)

    masters = nodes // blk
    with scope("buildf"):

        def build_rows(i, _):
            rows(adj, i)[...] = nt(rows(dst_hot, i)[...], src_hot[...]).astype(BF16)
            return 0

        lax.fori_loop(masters, masters + 1, build_rows, 0)

    with scope("bwait"):
        pl.semaphore_wait(barrier, n_dev - 1)
    exchange(0)

    with scope("prepg"):
        loads[1].wait()
        inv_row = 1.0 / jnp.maximum(in_count_ref[...], 1).astype(F32)
        inv_col = jnp.broadcast_to(inv_row, (128, nodes)).T
        inv[...] = jnp.concatenate([inv_col] * (dim // 128), axis=1)
        loads[7].wait()
        ybuf[...] = (cot[...].astype(F32) * inv[...]).astype(BF16)
        fill(1, nn(picks[...], ybuf[...]))
    exchange(1)

    with scope("buildm"):

        lax.fori_loop(masters + 1, slots // blk, build_rows, 0)

        def build_columns(i, _):
            here = pl.ds(pl.multiple_of(i * blk, blk), blk)
            adj[here, nodes:] = nt(dst_hot[here, :], src_hot[nodes:, :]).astype(BF16)
            return 0

        lax.fori_loop(0, masters, build_columns, 0)

    with scope("own1"):
        fown[nodes:, :] = nn(adj[nodes:, :nodes], feat[...])
        gown[nodes:, :] = tn(adj[:nodes, nodes:], ybuf[...])
        for c in loads[8:]:
            c.wait()
        zbuf[...] = nn(feat[...], wts[0]) + bias_ref[...]
        gbuf[...] = nt(cot[...], wts[2])

    fm = arrive(0)
    fill(2, fown[nodes:, :] + nn(adj[nodes:, nodes:], fm))
    exchange(2)
    gm = arrive(1)
    fill(3, gown[nodes:, :] + tn(adj[nodes:, nodes:], gm))
    exchange(3)

    with scope("buildo"):

        def build_rest(i, _):
            here = pl.ds(pl.multiple_of(i * blk, blk), blk)
            adj[here, :nodes] = nt(dst_hot[here, :], src_hot[:nodes, :]).astype(BF16)
            return 0

        lax.fori_loop(0, masters, build_rest, 0)
    with scope("own2"):
        fown[:nodes, :] = nn(adj[:nodes, :nodes], feat[...]) + nn(adj[:nodes, nodes:], fm)
        gown[:nodes, :] = tn(adj[:nodes, :nodes], ybuf[...]) + tn(adj[nodes:, :nodes], gm)

    big = nodes // 2
    fm2 = arrive(2)
    with scope("dense1"):
        for i in range(nodes // big):
            here = pl.ds(i * big, big)
            mean = ((fown[here, :] + nn(place[here, :], fm2)) * inv[here, :]).astype(BF16)
            mbuf[here, :] = mean
            z = zbuf[here, :] + nn(mean, wts[1])
            sig = 1.0 / (1.0 + jnp.exp(-z))
            hbuf[here, :] = (z * sig).astype(BF16)
            zbuf[here, :] = sig * (1.0 + z * (1.0 - sig))
        wpart[pl.ds(2 * dim, dim), :] = tn(hbuf[...], cot[...])

    gm2 = arrive(3)
    with scope("dense2"):
        bias_sum = jnp.zeros((1, dim), F32)
        for i in range(nodes // big):
            here = pl.ds(i * big, big)
            gsum = (gown[here, :] + nn(place[here, :], gm2)).astype(BF16)
            gsbuf[here, :] = gsum
            gh = gbuf[here, :] + nt(gsum, wts[3])
            gz = (gh * zbuf[here, :]).astype(BF16)
            gzbuf[here, :] = gz
            gzf = gz.astype(F32)
            ybuf[here, :] = (gzf * inv[here, :]).astype(BF16)
            bias_sum += jnp.sum(gzf, axis=0, keepdims=True)
        bpart[...] = bias_sum

    with scope("pick3"):
        fill(4, nn(picks[...], ybuf[...]))
    exchange(4)

    with scope("wgrad"):
        wpart[pl.ds(0, dim), :] = tn(feat[...], gzbuf[...])
        wpart[pl.ds(dim, dim), :] = tn(mbuf[...], gzbuf[...])
        wpart[pl.ds(3 * dim, dim), :] = tn(hbuf[...], gsbuf[...])
    mine = pl.ds(pl.multiple_of(core * half, half), half)
    other = pl.ds(pl.multiple_of((1 - core) * half, half), half)
    wsend[...] = wpart[other, :].astype(BF16)
    pair_w = pltpu.make_async_remote_copy(
        src_ref=wsend,
        dst_ref=wpair,
        send_sem=ssem.at[6],
        recv_sem=rsem.at[6],
        device_id=partner,
        device_id_type=MESH,
    )
    pair_b = pltpu.make_async_remote_copy(
        src_ref=bpart,
        dst_ref=bpair,
        send_sem=ssem.at[7],
        recv_sem=rsem.at[7],
        device_id=partner,
        device_id_type=MESH,
    )
    pair_w.start()
    pair_b.start()

    with scope("own3"):
        hown[...] = tn(adj[:nodes, :], ybuf[...])

    with scope("pairwait"):
        pair_w.wait()
        pair_b.wait()
    rs_send[...] = (wpart[mine, :] + wpair[...].astype(F32)).astype(rs_send.dtype).reshape(rs_send.shape)
    bias_pair = bpart[...] + bpair[...]

    places = (at_x, at_z, at_y)

    def bias_out(stage, value):
        bsum[stage] = value
        brecv[stage, places[stage]] = value
        for k in (2, 1, 3):
            to = (
                (d, wrap4(at_x + k) * 2 + core),
                (at_y * 4 + wrap4(at_z + k), s),
                (wrap4(at_y + k) * 4 + at_z, s),
            )[stage]
            pltpu.make_async_remote_copy(
                src_ref=bsum.at[stage],
                dst_ref=brecv.at[stage, places[stage]],
                send_sem=bsem.at[0, stage],
                recv_sem=bsem.at[1, stage],
                device_id=to,
                device_id_type=MESH,
            ).start()

    def bias_in(stage):
        others = brecv.at[stage, pl.ds(0, 3)]
        pltpu.make_async_copy(others, others, bsem.at[1, stage]).wait()
        return jnp.sum(brecv[stage], axis=0)

    def scatter(a, b):
        pltpu.make_async_remote_copy(
            src_ref=rs_send.at[lax.div(a * n_sub + b, 2)],
            dst_ref=rs_recv.at[chip],
            send_sem=ssem.at[8],
            recv_sem=rsem.at[8],
            device_id=(a, b),
            device_id_type=MESH,
        ).start()

    bias_out(0, bias_pair)
    with scope("scatter"):
        each(scatter, False)
        own_rs = pltpu.make_async_copy(rs_send.at[chip], rs_recv.at[chip], loc_sem.at[6])
        own_rs.start()

    hm = arrive(4)
    bias_out(1, bias_in(0))
    fill(5, hown[nodes:, :] + tn(adj[nodes:, nodes:], hm))
    exchange(5)
    with scope("own4"):
        hown[:nodes, :] += tn(adj[nodes:, :nodes], hm)
        zbuf[...] = nt(gzbuf[...], wts[0])

    with scope("rswait"):
        own_rs.wait()
        others = rs_recv.at[pl.ds(0, n_chip - 1)]
        pltpu.make_async_copy(others, others, rsem.at[8]).wait()
    ag_send[...] = (jnp.sum(rs_recv[...].astype(F32), axis=0) * norm_factor).astype(ag_send.dtype)

    def gather(a, b):
        pltpu.make_async_remote_copy(
            src_ref=ag_send,
            dst_ref=ag_all.at[core, chip],
            send_sem=ssem.at[10],
            recv_sem=rsem.at[10],
            device_id=(a, b),
            device_id_type=MESH,
        ).start()

    bias_out(2, bias_in(1))
    with scope("gather"):
        each(gather, False)
        own_ag = pltpu.make_async_copy(ag_send, ag_all.at[core, chip], loc_sem.at[8])
        own_ag.start()

    hm2 = arrive(5)
    with scope("last"):

        for i in range(nodes // big):
            here = pl.ds(i * big, big)
            hsum = (hown[here, :] + nn(place[here, :], hm2)).astype(BF16)
            gfeat_ref[here, :] = (zbuf[here, :] + nt(hsum, wts[1])).astype(BF16)

    with scope("agwait"):
        own_ag.wait()
        others = ag_all.at[core, pl.ds(0, n_chip - 1)]
        pltpu.make_async_copy(others, others, rsem.at[10]).wait()
    swap = pltpu.make_async_remote_copy(
        src_ref=ag_all.at[core],
        dst_ref=ag_all.at[core],
        send_sem=ssem.at[11],
        recv_sem=rsem.at[11],
        device_id=partner,
        device_id_type=MESH,
    )
    with scope("swap"):
        swap.start()
        gb_ref[...] = bias_in(2) * norm_factor
        swap.wait()
    gw_ref[...] = ag_all[...].astype(F32).reshape(4 * dim, dim)

    with scope("drain"):
        for k in range(6):
            sent(k)
        others = rs_send.at[pl.ds(0, n_chip - 1)]
        pltpu.make_async_copy(others, others, ssem.at[8]).wait()
        for stage in range(3):
            others = brecv.at[stage, pl.ds(0, 3)]
            pltpu.make_async_copy(others, others, bsem.at[0, stage]).wait()
        others = ag_all.at[core, pl.ds(0, n_chip - 1)]
        pltpu.make_async_copy(others, others, ssem.at[10]).wait()


def put(*refs):
    sem = refs[-1]
    half = len(refs) // 2
    copies = [
        pltpu.make_async_copy(a, b, sem.at[i])
        for i, (a, b) in enumerate(zip(refs[:half], refs[half:-1]))
    ]
    for c in copies:
        c.start()
    for c in copies:
        c.wait()


def shards(
    n_dom,
    n_sub,
    features,
    cotangent,
    w_self_one,
    w_nbr_one,
    bias_one,
    w_self_two,
    w_nbr_two,
    in_count,
    send_list,
    src_slot,
    dst_slot,
    edge_count,
):
    nodes, dim = features.shape
    n_dev = n_dom * n_sub
    n_chip = n_dev // 2
    per_peer = send_list.shape[2]
    n_mir = n_dev * per_peer
    slots = nodes + n_mir
    edges = src_slot.shape[1]
    own_rows = 2 * dim // n_chip
    vm = pl.BlockSpec(memory_space=pltpu.VMEM)
    hbm = pl.BlockSpec(memory_space=pltpu.HBM)
    norm_factor = float(nodes * n_dev) ** -0.5
    full = pltpu.VMEM((nodes, dim), F32)
    fullb = pltpu.VMEM((nodes, dim), BF16)
    allf = pltpu.VMEM((slots, dim), F32)
    msgs = pltpu.VMEM((6, n_dev, per_peer, dim), BF16)
    rs_t = BF16
    ag_t = BF16
    gfeat, gw, gb = pl.pallas_call(
        functools.partial(kernel, n_dom, n_sub, norm_factor),
        out_shape=(
            jax.ShapeDtypeStruct((nodes, dim), BF16),
            jax.ShapeDtypeStruct((4 * dim, dim), F32),
            jax.ShapeDtypeStruct((1, dim), F32),
        ),
        in_specs=[hbm] * 12,
        out_specs=(vm, vm, vm),
        scratch_shapes=[
            pltpu.VMEM((1, 1), jnp.int32),
            pltpu.VMEM((1, edges), jnp.int32),
            pltpu.VMEM((1, edges), jnp.int32),
            pltpu.VMEM((per_peer, n_dev), jnp.int32),
            pltpu.VMEM((1, nodes), jnp.int32),
            pltpu.VMEM((1, dim), F32),
            fullb,
            fullb,
            pltpu.VMEM((4, dim, dim), BF16),
            pltpu.VMEM((slots, edges), ONE_HOT),
            pltpu.VMEM((slots, edges), ONE_HOT),
            pltpu.VMEM((slots, slots), BF16),
            pltpu.VMEM((nodes, n_mir), BF16),
            pltpu.VMEM((n_mir, nodes), BF16),
            full,
            fullb,
            full,
            full,
            allf,
            allf,
            allf,
            fullb,
            fullb,
            fullb,
            fullb,
            msgs,
            msgs,
            pltpu.VMEM((4 * dim, dim), F32),
            pltpu.VMEM((1, dim), F32),
            pltpu.VMEM((2 * dim, dim), BF16),
            pltpu.VMEM((2 * dim, dim), BF16),
            pltpu.VMEM((1, dim), F32),
            pltpu.VMEM((3, 1, dim), F32),
            pltpu.VMEM((3, 4, 1, dim), F32),
            pltpu.VMEM((n_chip, own_rows, dim), rs_t),
            pltpu.VMEM((n_chip, own_rows, dim), rs_t),
            pltpu.VMEM((own_rows, dim), ag_t),
            pltpu.VMEM((2, n_chip, own_rows, dim), ag_t),
            pltpu.SemaphoreType.DMA((12,)),
            pltpu.SemaphoreType.DMA((9,)),
            pltpu.SemaphoreType.DMA((12,)),
            pltpu.SemaphoreType.DMA((12,)),
            pltpu.SemaphoreType.DMA((2, 3)),
        ],
        compiler_params=pltpu.CompilerParams(
            collective_id=0, has_side_effects=True, vmem_limit_bytes=44 << 20
        ),
    )(
        edge_count.reshape(1, 1),
        *(
            pltpu.with_memory_space_constraint(x, pltpu.HBM)
            for x in (
                src_slot,
                dst_slot,
                send_list[0].T,
                in_count.reshape(1, nodes),
                bias_one.reshape(1, dim),
                features,
                cotangent,
                w_self_one,
                w_nbr_one,
                w_self_two,
                w_nbr_two,
            )
        ),
    )
    results = (gfeat, gw, gb)
    gfeat, gw, gb = pl.pallas_call(
        put,
        out_shape=tuple(jax.ShapeDtypeStruct(x.shape, x.dtype) for x in results),
        in_specs=[vm] * 3,
        out_specs=(hbm,) * 3,
        scratch_shapes=[pltpu.SemaphoreType.DMA((3,))],
        compiler_params=pltpu.CompilerParams(vmem_limit_bytes=1 << 20),
    )(*results)
    return gfeat, gw.reshape(4, dim, dim), gb.reshape(dim)


def solution(mesh):
    both = ("dom", "sub")
    return jax.shard_map(
        functools.partial(shards, mesh.shape["dom"], mesh.shape["sub"]),
        mesh=mesh,
        in_specs=(
            P(both, None),
            P(both, None),
            P(),
            P(),
            P(),
            P(),
            P(),
            P(both),
            P(both, None, None),
            P(both, None),
            P(both, None),
            P(both),
        ),
        out_specs=(P(both, None), P(), P()),
        check_vma=False,
    )
```
